32 devices in a mesh: win: 2 (over x), tile: 16 (over z, y, core).
Axes of the slice: x: 2, y: 2, z: 4, core: 2. Of those that a mesh axis runs over, the one named last changes fastest.
Arguments:
- mask: float32 [512, 4096], P('win', 'tile'), parts along dimension 0, may hold values from -1 to 1
- target: float32 [512, 4096], P('win', 'tile'), parts along dimension 0, may hold values from 0 to 1
- kernel_table: float32 [4, 2, 2, 64, 64], replicated, may hold values from -48 to 48
- kernel_weight: float32 [4, 2], replicated, may hold values from 0.25 to 1
- dose_table: float32 [4], replicated, may hold values from 0.7 to 1.4
- condition_index: int32 [2], replicated, may hold values from 0 to 3, as said below
Outputs:
- resist: float32 [2, 512, 4096], P(None, 'win', 'tile'), parts along dimension 1
- gradient: float32 [512, 4096], P('win', 'tile'), parts along dimension 0
The draws below stay inside these ranges and needn't reach their ends.
There are 2 independent parts, one for each index of `win`. The reference program is written for one: setup_inputs(seed, part) draws one part's arguments, and reference() takes and returns one part's arrays. A program takes and returns all parts, laid end to end along the dimension named above; an argument that names none is the same for every part. Nothing has to cross between parts.
Inputs may be any that keep to these rules, and one draw needn't show every extreme that they name: `condition_index`: the 2 entries are distinct table indices.
All inputs are finite; a program needn't handle non-finite values.
Results may differ from the reference program's by a relative error of at most 0.00015.
Values sent between devices are 32-bit elements; how exact they have to be, the bound alone decides.
No kernel may reach another device: no remote copies, remote signals or barrier semaphores. Data moves between devices by JAX's collectives and lax.ppermute only.
A program may use at most 64 MiB of HBM per device.

```python
import math
import jax
import jax.numpy as jnp
from jax import lax

NPAD = 512
MARGIN = 128
BAND = 64
KERN = 2
CONDS = 2
TABLE = 4
TROWS = 1
CORE = 256
ROWS = 256
COLS = 4096


def draw_condition_index(key, part):
    order_key = jax.random.fold_in(key, 11)
    slot_key = jax.random.fold_in(key, 23)
    chosen = jax.random.permutation(order_key, jnp.arange(TABLE - 1, dtype=jnp.int32))
    chosen = jnp.concatenate([chosen, jnp.zeros((1,), jnp.int32)])[:CONDS]
    slot = jax.random.randint(slot_key, (), 0, CONDS, dtype=jnp.int32)
    places = jnp.arange(CONDS, dtype=jnp.int32)
    return jnp.where(places == slot, jnp.int32(TABLE - 1), chosen).astype(jnp.int32)


def shard_levels(stream_key, extent, pieces, low, high):
    factor_of = 1.0
    for dim, blocks in pieces:
        heights = jax.random.uniform(jax.random.fold_in(jax.random.fold_in(stream_key, 6), dim), (blocks,), jnp.float32, low / len(pieces), high / len(pieces))
        factor_of = factor_of * jnp.repeat(jnp.exp(heights), extent[dim] // blocks).reshape((-1,) + (1,) * (len(extent) - 1 - dim))
    return factor_of


def gaussian(key, dims, spread, most, held_as=jnp.bfloat16):
    entries = jax.random.normal(key, dims, jnp.float32) * spread
    return jnp.minimum(jnp.maximum(entries, -most), most).astype(held_as)


def setup_inputs(seed: int = 0, part: int = 0) -> dict:
    arg_keys = jax.random.split(jax.random.key(seed), 7)
    own_keys = jax.random.split(jax.random.fold_in(arg_keys[6], part), 7)
    mask = jnp.clip(jax.random.uniform(own_keys[0], (ROWS, COLS), jnp.float32, -1.0, 1.0) * shard_levels(own_keys[0], (ROWS, COLS), ((1, 16),), -0.4, 0.0), -1.0, 1.0)
    target = jnp.clip(1.0 * jax.random.uniform(own_keys[1], (ROWS, COLS), jnp.float32) ** shard_levels(own_keys[1], (ROWS, COLS), ((1, 16),), -0.2, 0.2), 0.0, 1.0)
    kernel_table = gaussian(arg_keys[2], (TABLE, KERN, 2, BAND, BAND), (NPAD // BAND), 48.0, jnp.float32)
    kernel_weight = jnp.clip(jnp.exp(jax.random.uniform(arg_keys[3], (TABLE, KERN), jnp.float32, math.log(0.25), math.log(1.0))), 0.25, 1.0)
    dose_table = jnp.clip(jax.random.uniform(arg_keys[4], (TABLE,), jnp.float32, 0.7, 1.4), 0.7, 1.4)
    condition_index = draw_condition_index(jax.random.fold_in(arg_keys[6], 71), part)
    return {"mask": mask, "target": target, "kernel_table": kernel_table, "kernel_weight": kernel_weight, "dose_table": dose_table, "condition_index": condition_index}


highest = lax.Precision.HIGHEST
steepness = 6.0
threshold = 0.3

def product(left, right):
    return jnp.matmul(left, right, precision=highest)

def band_tables():
    frequency = jnp.arange(BAND, dtype=jnp.int32) - BAND // 2
    position = jnp.arange(NPAD, dtype=jnp.int32)
    phase = (frequency[:, None] * position[None, :] % NPAD).astype(jnp.float32) * (2.0 * math.pi / NPAD)
    return (jnp.cos(phase), -jnp.sin(phase))

def select_conditions(kernel_table, kernel_weight, dose_table, condition_index):
    selector = (condition_index[:, None] == jnp.arange(TABLE, dtype=jnp.int32)[None, :]).astype(jnp.float32)
    kernels = jnp.einsum('ct,tkrab->ckrab', selector, kernel_table, precision=highest)
    return (kernels, product(selector, kernel_weight), product(selector, dose_table))

def column_pass(frames, cosine, sine):
    return (product(frames, cosine.T), product(frames, sine.T))

def row_pass(real, imaginary, cosine, sine):
    first = product(cosine, real) - product(sine, imaginary)
    second = product(cosine, imaginary) + product(sine, real)
    return (first / NPAD, second / NPAD)

def synthesize(real, imaginary, cosine, sine):
    first = product(real, cosine) + product(imaginary, sine)
    second = product(imaginary, cosine) - product(real, sine)
    out_real = (product(cosine.T, first) + product(sine.T, second)) / NPAD
    out_imaginary = (product(cosine.T, second) - product(sine.T, first)) / NPAD
    return (out_real, out_imaginary)

def tile_terms(frames, goals, kernels, weights, doses, cosine, sine):
    spec_real, spec_imaginary = row_pass(*column_pass(frames, cosine, sine), cosine, sine)
    loss = jnp.zeros((), jnp.float32)
    printed = []
    for condition in range(CONDS):
        kernel_real = kernels[condition, :, 0]
        kernel_imaginary = kernels[condition, :, 1]
        mixed_real = kernel_real * spec_real[:, None] - kernel_imaginary * spec_imaginary[:, None]
        mixed_imaginary = kernel_real * spec_imaginary[:, None] + kernel_imaginary * spec_real[:, None]
        field_real, field_imaginary = synthesize(mixed_real, mixed_imaginary, cosine, sine)
        power = field_real * field_real + field_imaginary * field_imaginary
        intensity = jnp.einsum('k,tkmn->tmn', weights[condition], power, precision=highest)
        image = jax.nn.sigmoid(steepness * (doses[condition] * intensity - threshold))
        inner = image[:, MARGIN:MARGIN + CORE, MARGIN:MARGIN + CORE]
        loss = loss + 2.0 * jnp.sum((inner - goals) * (inner - goals))
        printed.append(inner)
    return (loss, jnp.stack(printed))

def reference(mask, target, kernel_table, kernel_weight, dose_table, condition_index):
    cosine, sine = band_tables()
    kernels, weights, doses = select_conditions(kernel_table, kernel_weight, dose_table, condition_index)

    def total(window):
        extended = jnp.pad(window, MARGIN)

        def strip_terms(column):
            start = column * CORE
            strip = lax.dynamic_slice(extended, (jnp.int32(0), start), (ROWS + 2 * MARGIN, NPAD))
            frames = jnp.stack([strip[row * CORE:row * CORE + NPAD] for row in range(TROWS)])
            goals = lax.dynamic_slice(target, (jnp.int32(0), start), (ROWS, CORE)).reshape(TROWS, CORE, CORE)
            return tile_terms(frames, goals, kernels, weights, doses, cosine, sine)
        losses, printed = lax.map(jax.checkpoint(strip_terms), jnp.arange(COLS // CORE, dtype=jnp.int32))
        return (jnp.sum(losses), printed)
    loss, pullback, printed = jax.vjp(total, mask, has_aux=True)
    gradient = pullback(jnp.ones_like(loss))[0]
    resist = jnp.transpose(printed, (1, 2, 3, 0, 4)).reshape(CONDS, ROWS, COLS)
    return (resist, gradient)
```

```python
import math

import jax
import jax.numpy as jnp
import ml_dtypes
import numpy as np
from jax import lax
from jax.experimental import pallas as pl
from jax.experimental.pallas import tpu as pltpu
from jax.sharding import PartitionSpec as P

NPAD = 512
MARGIN = 128
BAND = 64
KERN = 2
CONDS = 2
CORE = 256
PAIRS = CONDS * KERN
WIDE = 2 * BAND

steepness = 6.0
threshold = 0.3


def parts(table):
    high = table.astype(ml_dtypes.bfloat16)
    low = (table - high.astype(np.float64)).astype(ml_dtypes.bfloat16)
    return high, low


def tables():
    frequency = np.arange(BAND)[:, None] - BAND // 2
    position = np.arange(MARGIN, MARGIN + CORE)[None, :]
    phase = (frequency * position % NPAD) * (2.0 * math.pi / NPAD)
    cosine, sine = np.cos(phase), -np.sin(phase)
    rows = np.concatenate([cosine, sine], 0)
    half = CORE // 2
    split = np.zeros((CORE, CORE))
    split[:half, :WIDE] = rows[:, :half].T
    split[half:, WIDE:] = rows[:, half:].T
    out = np.block([[cosine, -sine], [sine, cosine]])
    back = np.block([[cosine.T, sine.T], [-sine.T, cosine.T]])
    return rows, split, out, back


def side_by_side(pair, axis):
    return np.concatenate(pair, axis)


def halves(x):
    high = x.astype(jnp.bfloat16)
    return high, (x - high.astype(jnp.float32)).astype(jnp.bfloat16)


def dot(a, b):
    return jnp.dot(a, b, preferred_element_type=jnp.float32)


def turn(x):
    lane = lax.broadcasted_iota(jnp.int32, x.shape, 1)
    rolled = pltpu.roll(x, BAND, 1)
    return jnp.where(lane < BAND, -rolled, rolled)


def signs(shape):
    lane = lax.broadcasted_iota(jnp.int32, shape, 1)
    return jnp.where(lane % 2 == 0, 1.0, -1.0).astype(jnp.float32)


def stacked(x):
    return jnp.concatenate([x, -turn(x)], 0)


def analyze_kernel(mask, rows, split_high, split_low, own, even_out, odd_out):
    odd = lax.axis_index("tile") % 2 == 1
    high, low = halves(mask[...])
    both = dot(rows[...], high)
    z = both[:WIDE] + both[WIDE:] + dot(rows[:WIDE], low)
    z_high, z_low = halves(z)
    w = (
        dot(z_high, split_high[...])
        + dot(z_low, split_high[...])
        + dot(z_high, split_low[...])
    )
    left = w[:BAND, :WIDE] + turn(w[BAND:, :WIDE])
    right = w[:BAND, WIDE:] + turn(w[BAND:, WIDE:])
    own[...] = left + right
    sign = signs(left.shape)
    left = left * sign
    right = right * sign
    even_out[...] = jnp.where(odd, left, right)
    odd_out[...] = jnp.where(odd, right, left)


def prepare_kernel(index, weight, dose, table, mixed):
    for condition in range(CONDS):
        entry = index[condition]
        for k in range(KERN):
            scale = jnp.sqrt(
                jnp.full((1, WIDE), 0.5 * steepness * dose[entry] * weight[entry, k])
            ) * (1.0 / (NPAD * NPAD))
            for part in range(2):
                kernel = table[entry, k, part]
                doubled = jnp.concatenate([kernel, kernel], 1)
                mixed[condition * KERN + k, part] = doubled * scale


def window_kernel(
    own, even_in, odd_in, target, mixed, rows_t, rows, out_high, out_low, back_both, back_high,
    resist, grad, field,
):
    tile, tiles = lax.axis_index("tile"), lax.axis_size("tile")
    alone = jnp.logical_or(tile == 0, tile == tiles - 1)
    spec = own[...] + even_in[...] + jnp.where(alone, 0.0, odd_in[...])
    turned = turn(spec)
    stack = jnp.concatenate(
        [stacked(mixed[i, 0] * spec + mixed[i, 1] * turned) for i in range(PAIRS)], 1
    )
    high, low = halves(stack)
    first = dot(rows_t[...], jnp.concatenate([high, high], 0)) + dot(rows_t[:, :WIDE], low)
    y_high, y_low = halves(first)
    half = CORE // 2
    q_parts = [[None, None] for _ in range(PAIRS)]
    for condition in range(CONDS):
        for part in range(2):
            r = slice(part * half, (part + 1) * half)
            cols = [slice((condition * KERN + k) * WIDE, (condition * KERN + k + 1) * WIDE) for k in range(KERN)]
            a = jnp.concatenate([y_high[r, c] for c in cols], 0)
            b = jnp.concatenate([y_low[r, c] for c in cols], 0)
            f = dot(jnp.concatenate([a, b], 1), out_high[...]) + dot(a, out_low[...])
            squares = f * f
            power = squares[:half, :CORE] + squares[:half, CORE:] + squares[half:, :CORE] + squares[half:, CORE:]
            t = jnp.tanh(power - 0.5 * steepness * threshold)
            resist[condition, r] = 0.5 + 0.5 * t
            drive = (t + (1.0 - 2.0 * target[r])) * (2.0 - 2.0 * (t * t))
            scaled = jnp.concatenate([drive, drive], 1)
            scaled = jnp.concatenate([scaled, scaled], 0) * f
            s_high, s_low = halves(scaled)
            both = dot(s_high, back_both[...])
            q = both[:, :WIDE] + both[:, WIDE:] + dot(s_low, back_high[...])
            for k in range(KERN):
                q_parts[condition * KERN + k][part] = q[k * half : (k + 1) * half]
    q = jnp.concatenate([jnp.concatenate(p, 0) for p in q_parts], 1)
    q_high, q_low = halves(q)
    both = dot(rows[...], q_high)
    u = both[:WIDE] + both[WIDE:] + dot(rows[:WIDE], q_low)
    total = jnp.zeros((BAND, WIDE), jnp.float32)
    for i in range(PAIRS):
        c = slice(i * WIDE, (i + 1) * WIDE)
        back = u[:BAND, c] + turn(u[BAND:, c])
        total = total + mixed[i, 0] * back - mixed[i, 1] * turn(back)
    grad[...] = total


def synthesize_kernel(own, even_in, odd_in, rows_t, split_high, split_low, gradient):
    tile, tiles = lax.axis_index("tile"), lax.axis_size("tile")
    odd = tile % 2 == 1
    alone = jnp.logical_or(tile == 0, tile == tiles - 1)
    sign = signs((BAND, WIDE))
    beside = even_in[...] * sign
    across = jnp.where(alone, 0.0, odd_in[...] * sign)
    left = own[...] + jnp.where(odd, beside, across)
    right = own[...] + jnp.where(odd, across, beside)
    stack = jnp.concatenate([stacked(left), stacked(right)], 1)
    high, low = halves(stack)
    y = dot(rows_t[...], jnp.concatenate([high, high], 0)) + dot(rows_t[:, :WIDE], low)
    y_high, y_low = halves(y)
    gradient[...] = (
        dot(y_high, split_high[...])
        + dot(y_low, split_high[...])
        + dot(y_high, split_low[...])
    )


def call(kernel, outs, scratch=(), smem=0, n=0, flops=0):
    spec = [pl.BlockSpec(memory_space=pltpu.SMEM)] * smem + [
        pl.BlockSpec(memory_space=pltpu.VMEM)
    ] * (n - smem)
    shapes = [jax.ShapeDtypeStruct(o, jnp.float32) for o in outs]
    return pl.pallas_call(
        kernel,
        out_shape=shapes if len(shapes) > 1 else shapes[0],
        in_specs=spec,
        out_specs=[pl.BlockSpec(memory_space=pltpu.VMEM)] * len(outs)
        if len(outs) > 1
        else pl.BlockSpec(memory_space=pltpu.VMEM),
        scratch_shapes=list(scratch),
        compiler_params=pltpu.CompilerParams(vmem_limit_bytes=16 << 20),
        cost_estimate=pl.CostEstimate(flops=flops, bytes_accessed=1 << 20, transcendentals=0),
    )


def partners(windows, tiles):
    even = [(w * tiles + i, w * tiles + (i ^ 1)) for w in range(windows) for i in range(tiles)]
    odd = []
    for w in range(windows):
        base = w * tiles
        for i in range(1, tiles - 1, 2):
            odd += [(base + i, base + i + 1), (base + i + 1, base + i)]
        other = w ^ 1 if (w ^ 1) < windows else w
        for i in (0, tiles - 1):
            odd.append((base + i, other * tiles + i))
    return even, odd


def local(mask, target, kernel_table, kernel_weight, dose_table, condition_index):
    rows, split, out, back = tables()
    rows_high, rows_low = parts(rows)
    rows_both = side_by_side((rows_high, rows_low), 0)
    rows_t = np.ascontiguousarray(rows_both.T)
    split_high, split_low = parts(split)
    split_t_high, split_t_low = (np.ascontiguousarray(s.T) for s in (split_high, split_low))
    out_high, out_low = parts(out)
    back_high, back_low = parts(back)
    out_twice = side_by_side((out_high, out_high), 0)
    back_both = side_by_side((back_high, back_low), 1)
    even, odd = partners(lax.axis_size("win"), lax.axis_size("tile"))

    def swap(x, y):
        over = ("win", "tile")
        b = lax.ppermute(y, over, odd)
        a = lax.ppermute(x, over, even)
        return a, b

    small = (BAND, WIDE)
    own, to_even, to_odd = call(analyze_kernel, [small] * 3, n=4, flops=10**8)(
        mask, rows_both, split_high, split_low
    )
    mixed = call(prepare_kernel, [(PAIRS, 2, BAND, WIDE)], smem=3, n=4, flops=10**6)(
        condition_index, kernel_weight, dose_table, kernel_table
    )
    from_even, from_odd = swap(to_even, to_odd)
    resist, grad = call(
        window_kernel,
        [(CONDS, CORE, CORE), small],
        scratch=[pltpu.VMEM((8, 128), jnp.float32)],
        n=11,
        flops=10**9,
    )(own, from_even, from_odd, target, mixed, rows_t, rows_both, out_twice, out_low, back_both, back_high)
    from_even, from_odd = swap(grad, grad)
    gradient = call(synthesize_kernel, [(CORE, CORE)], n=6, flops=10**8)(
        grad, from_even, from_odd, rows_t, split_t_high, split_t_low
    )
    return (resist, gradient)


def solution(mesh):
    return jax.shard_map(
        local,
        mesh=mesh,
        in_specs=(P("win", "tile"), P("win", "tile"), P(), P(), P(), P()),
        out_specs=(P(None, "win", "tile"), P("win", "tile")),
        check_vma=False,
    )
```

```python
import math

import jax
import jax.numpy as jnp
import ml_dtypes
import numpy as np
from jax import lax
from jax.experimental import pallas as pl
from jax.experimental.pallas import tpu as pltpu
from jax.sharding import PartitionSpec as P

NPAD = 512
MARGIN = 128
BAND = 64
KERN = 2
CONDS = 2
CORE = 256
PAIRS = CONDS * KERN
WIDE = 2 * BAND

steepness = 6.0
threshold = 0.3


def parts(table):
    high = table.astype(ml_dtypes.bfloat16)
    low = (table - high.astype(np.float64)).astype(ml_dtypes.bfloat16)
    return high, low


def tables():
    frequency = np.arange(BAND)[:, None] - BAND // 2
    position = np.arange(MARGIN, MARGIN + CORE)[None, :]
    phase = (frequency * position % NPAD) * (2.0 * math.pi / NPAD)
    cosine, sine = np.cos(phase), -np.sin(phase)
    rows = np.concatenate([cosine, sine], 0)
    out = np.block([[cosine, -sine], [sine, cosine]])
    back = np.block([[cosine.T, sine.T], [-sine.T, cosine.T]])
    return rows, out, back


def halves(x):
    high = x.astype(jnp.bfloat16)
    return high, (x - high.astype(jnp.float32)).astype(jnp.bfloat16)


def dot(a, b):
    return jnp.dot(a, b, preferred_element_type=jnp.float32)


def turn(x):
    lane = lax.broadcasted_iota(jnp.int32, x.shape, 1)
    rolled = pltpu.roll(x, BAND, 1)
    return jnp.where(lane < BAND, -rolled, rolled)


def signs(shape):
    lane = lax.broadcasted_iota(jnp.int32, shape, 1)
    return jnp.where(lane % 2 == 0, 1.0, -1.0).astype(jnp.float32)


def stacked(x):
    return jnp.concatenate([x, -turn(x)], 0)


def copies(pairs, sems):
    moves = [pltpu.make_async_copy(a, b, sems.at[i]) for i, (a, b) in enumerate(pairs)]
    for move in moves:
        move.start()
    return moves


def place():
    tile, tiles = lax.axis_index("tile"), lax.axis_size("tile")
    return tile % 2 == 1, jnp.logical_or(tile == 0, tile == tiles - 1)


def analyze_kernel(mask_hbm, rows_hbm, rows_t_hbm, own, even_out, odd_out, rows, rows_t, mask, sems):
    moves = copies([(mask_hbm, mask), (rows_hbm, rows), (rows_t_hbm, rows_t)], sems)
    for move in moves:
        move.wait()
    odd, _ = place()
    high, low = halves(mask[...])
    both = dot(rows[...], high)
    z = both[:WIDE] + both[WIDE:] + dot(rows[:WIDE], low)
    z_high, z_low = halves(z)
    z_both = jnp.concatenate([z_high, z_low], 0)
    sides = []
    for side in range(2):
        c = slice(side * MARGIN, (side + 1) * MARGIN)
        both = dot(z_both[:, c], rows_t[c, :WIDE])
        w = both[:WIDE] + both[WIDE:] + dot(z_high[:, c], rows_t[c, WIDE:])
        sides.append(w[:BAND] + turn(w[BAND:]))
    left, right = sides
    own[...] = left + right
    sign = signs(left.shape)
    left = left * sign
    right = right * sign
    even_out[...] = jnp.where(odd, left, right)
    odd_out[...] = jnp.where(odd, right, left)


def prepare_kernel(
    index, weight, dose, after, table_hbm, target_hbm, out_high_hbm, out_low_hbm, back_hbm,
    mixed, target, out_high, out_low, back, table, sems,
):
    moves = copies(
        [(table_hbm.at[index[c]], table.at[c]) for c in range(CONDS)]
        + [
            (target_hbm, target),
            (out_high_hbm, out_high),
            (out_low_hbm, out_low),
            (back_hbm, back),
        ],
        sems,
    )
    for condition in range(CONDS):
        entry = index[condition]
        moves[condition].wait()
        for k in range(KERN):
            scale = jnp.sqrt(
                jnp.full((1, WIDE), 0.5 * steepness * dose[entry] * weight[k, entry])
            ) * (1.0 / (NPAD * NPAD))
            for part in range(2):
                kernel = table[condition, k, part]
                doubled = jnp.concatenate([kernel, kernel], 1)
                mixed[condition * KERN + k, part] = doubled * scale
    for move in moves[CONDS:]:
        move.wait()


def window_kernel(
    own, even_in, odd_in, target, mixed, rows_t, rows, out_high, out_low, back_both,
    resist, grad,
):
    _, alone = place()
    spec = own[...] + even_in[...] + jnp.where(alone, 0.0, odd_in[...])
    turned = turn(spec)
    stack = jnp.concatenate(
        [stacked(mixed[i, 0] * spec + mixed[i, 1] * turned) for i in range(PAIRS)], 1
    )
    high, low = halves(stack)
    first = dot(rows_t[...], jnp.concatenate([high, high], 0)) + dot(rows_t[:, :WIDE], low)
    y_high, y_low = halves(first)
    out_twice = jnp.concatenate([out_high[...], out_high[...]], 0)
    half = CORE // 2
    q_parts = [[None, None] for _ in range(PAIRS)]
    for condition in range(CONDS):
        for part in range(2):
            r = slice(part * half, (part + 1) * half)
            group = [condition * KERN + k for k in range(KERN)]
            cols = [slice(i * WIDE, (i + 1) * WIDE) for i in group]
            a = jnp.concatenate([y_high[r, c] for c in cols], 0)
            b = jnp.concatenate([y_low[r, c] for c in cols], 0)
            f = dot(jnp.concatenate([a, b], 1), out_twice) + dot(a, out_low[...])
            squares = f * f
            power = sum(
                squares[k * half : (k + 1) * half, :CORE] + squares[k * half : (k + 1) * half, CORE:]
                for k in range(KERN)
            )
            t = jnp.tanh(power - 0.5 * steepness * threshold)
            resist[condition, r] = 0.5 + 0.5 * t
            drive = (t + (1.0 - 2.0 * target[r])) * (2.0 - 2.0 * (t * t))
            drive = jnp.concatenate([drive, drive], 1)
            scaled = jnp.concatenate([drive] * KERN, 0) * f
            s_high, s_low = halves(scaled)
            both = dot(s_high, back_both[...])
            q = both[:, :WIDE] + both[:, WIDE:] + dot(s_low, back_both[:, :WIDE])
            for k in range(KERN):
                q_parts[group[k]][part] = q[k * half : (k + 1) * half]
    q = jnp.concatenate([jnp.concatenate(p, 0) for p in q_parts], 1)
    q_high, q_low = halves(q)
    both = dot(rows[...], q_high)
    u = both[:WIDE] + both[WIDE:] + dot(rows[:WIDE], q_low)
    total = jnp.zeros((BAND, WIDE), jnp.float32)
    for i in range(PAIRS):
        c = slice(i * WIDE, (i + 1) * WIDE)
        back = u[:BAND, c] + turn(u[BAND:, c])
        total = total + mixed[i, 0] * back - mixed[i, 1] * turn(back)
    grad[...] = total


def synthesize(spec, rows, rows_t, side, out):
    high, low = halves(stacked(spec))
    y = dot(rows_t[...], jnp.concatenate([high, high], 0)) + dot(rows_t[:, :WIDE], low)
    y_high, y_low = halves(y)
    c = pl.ds(pl.multiple_of(side * MARGIN, MARGIN), MARGIN)
    both = dot(jnp.concatenate([y_high, y_low], 0), rows[:WIDE, c])
    out[...] = both[:CORE] + both[CORE:] + dot(y_high, rows[WIDE:, c])


def beside_kernel(own, even_in, rows, rows_t, resist, resist_hbm, gradient_hbm, out, sems):
    odd, _ = place()
    side = jnp.where(odd, 0, 1)
    first = copies([(resist, resist_hbm)], sems)[0]
    synthesize(own[...] + even_in[...] * signs((BAND, WIDE)), rows, rows_t, side, out)
    c = pl.ds(pl.multiple_of(side * MARGIN, MARGIN), MARGIN)
    second = pltpu.make_async_copy(out, gradient_hbm.at[:, c], sems.at[1])
    second.start()
    first.wait()
    second.wait()


def across_kernel(own, odd_in, rows, rows_t, half_hbm, gradient_hbm, out, sems):
    odd, alone = place()
    side = jnp.where(odd, 1, 0)
    extra = jnp.where(alone, 0.0, odd_in[...] * signs((BAND, WIDE)))
    synthesize(own[...] + extra, rows, rows_t, side, out)
    c = pl.ds(pl.multiple_of(side * MARGIN, MARGIN), MARGIN)
    move = pltpu.make_async_copy(out, gradient_hbm.at[:, c], sems.at[0])
    move.start()
    move.wait()


def pinned(*arrays):
    return [pltpu.with_memory_space_constraint(jnp.asarray(a), pltpu.HBM) for a in arrays]


SPACES = {"v": pltpu.VMEM, "h": pltpu.HBM, "s": pltpu.SMEM}


def call(kernel, ins, outs, scratch=(), aliases=None, flops=10**6):
    shapes = [jax.ShapeDtypeStruct(shape, dtype) for _, shape, dtype in outs]
    specs = [pl.BlockSpec(memory_space=SPACES[o[0]]) for o in outs]
    return pl.pallas_call(
        kernel,
        out_shape=shapes if len(shapes) > 1 else shapes[0],
        in_specs=[pl.BlockSpec(memory_space=SPACES[i]) for i in ins],
        out_specs=specs if len(specs) > 1 else specs[0],
        scratch_shapes=list(scratch),
        input_output_aliases=aliases or {},
        compiler_params=pltpu.CompilerParams(vmem_limit_bytes=16 << 20),
        cost_estimate=pl.CostEstimate(flops=flops, bytes_accessed=1 << 16, transcendentals=0),
    )


def partners(windows, tiles):
    even = [(w * tiles + i, w * tiles + (i ^ 1)) for w in range(windows) for i in range(tiles)]
    odd = []
    for w in range(windows):
        base = w * tiles
        for i in range(1, tiles - 1, 2):
            odd += [(base + i, base + i + 1), (base + i + 1, base + i)]
        other = w ^ 1 if (w ^ 1) < windows else w
        for i in (0, tiles - 1):
            odd.append((base + i, other * tiles + i))
    return even, odd


def local(mask, target, kernel_table, kernel_weight, dose_table, condition_index):
    rows, out, back = tables()
    rows_table = np.concatenate(parts(rows), 0)
    rows_t_table = np.ascontiguousarray(rows_table.T)
    out_high, out_low = parts(out)
    back_table = np.concatenate(parts(back), 1)
    even, odd = partners(lax.axis_size("win"), lax.axis_size("tile"))

    def swap(x, y):
        over = ("win", "tile")
        b = lax.ppermute(y, over, odd)
        a = lax.ppermute(x, over, even)
        return a, b

    f32, bf16 = jnp.float32, jnp.bfloat16
    small = ("v", (BAND, WIDE), f32)
    square = (CORE, CORE)
    dma = pltpu.SemaphoreType.DMA
    own, to_even, to_odd, rows, rows_t = call(
        analyze_kernel,
        "hhh",
        [small] * 3 + [("v", square, bf16)] * 2,
        [pltpu.VMEM(square, f32), dma((3,))],
    )(*pinned(mask, rows_table, rows_t_table))
    mixed, goal, out_high, out_low, back = call(
        prepare_kernel,
        "sss" + "v" + "hhhhh",
        [
            ("v", (PAIRS, 2, BAND, WIDE), f32),
            ("v", square, f32),
            ("v", out_high.shape, bf16),
            ("v", out_low.shape, bf16),
            ("v", back_table.shape, bf16),
        ],
        [pltpu.VMEM((CONDS, KERN, 2, BAND, BAND), f32), dma((CONDS + 4,))],
    )(
        condition_index, kernel_weight.T, dose_table, own,
        *pinned(kernel_table, target, out_high, out_low, back_table),
    )
    from_even, from_odd = swap(to_even, to_odd)
    resist, grad = call(
        window_kernel, "v" * 10, [("v", (CONDS, CORE, CORE), f32), small]
    )(own, from_even, from_odd, goal, mixed, rows_t, rows, out_high, out_low, back)
    from_even, from_odd = swap(grad, grad)
    strip = pltpu.VMEM((CORE, MARGIN), f32)
    resist, gradient = call(
        beside_kernel,
        "v" * 5,
        [("h", (CONDS, CORE, CORE), f32), ("h", square, f32)],
        [strip, dma((2,))],
    )(grad, from_even, rows, rows_t, resist)
    gradient = call(
        across_kernel, "vvvvh", [("h", square, f32)], [strip, dma((1,))], {4: 0}
    )(grad, from_odd, rows, rows_t, gradient)
    return (resist, gradient)


def solution(mesh):
    return jax.shard_map(
        local,
        mesh=mesh,
        in_specs=(P("win", "tile"), P("win", "tile"), P(), P(), P(), P()),
        out_specs=(P(None, "win", "tile"), P("win", "tile")),
        check_vma=False,
    )
```

```python
import math

import jax
import jax.numpy as jnp
import ml_dtypes
import numpy as np
from jax import lax
from jax.experimental import pallas as pl
from jax.experimental.pallas import tpu as pltpu
from jax.sharding import PartitionSpec as P

NPAD = 512
MARGIN = 128
BAND = 64
KERN = 2
TABLE = 4
CONDS = 2
CORE = 256
PAIRS = CONDS * KERN
WIDE = 2 * BAND
CHUNK = 64

steepness = 6.0
threshold = 0.3


def parts(table):
    high = table.astype(ml_dtypes.bfloat16)
    low = (table - high.astype(np.float64)).astype(ml_dtypes.bfloat16)
    return high, low


def tables():
    frequency = np.arange(BAND)[:, None] - BAND // 2
    position = np.arange(MARGIN, MARGIN + CORE)[None, :]
    phase = (frequency * position % NPAD) * (2.0 * math.pi / NPAD)
    cosine, sine = np.cos(phase), -np.sin(phase)
    rows = np.concatenate([cosine, sine], 0)
    return rows


def halves(x):
    high = x.astype(jnp.bfloat16)
    return high, (x - high.astype(jnp.float32)).astype(jnp.bfloat16)


def dot(a, b):
    return jnp.dot(a, b, preferred_element_type=jnp.float32)


def turn(x):
    lane = lax.broadcasted_iota(jnp.int32, x.shape, 1)
    rolled = pltpu.roll(x, BAND, 1)
    return jnp.where(lane < BAND, -rolled, rolled)


def signs(shape):
    lane = lax.broadcasted_iota(jnp.int32, shape, 1)
    return jnp.where(lane % 2 == 0, 1.0, -1.0).astype(jnp.float32)


def stacked(x):
    return jnp.concatenate([x, -turn(x)], 0)


def copies(pairs, sems):
    moves = [pltpu.make_async_copy(a, b, sems.at[i]) for i, (a, b) in enumerate(pairs)]
    for move in moves:
        move.start()
    return moves


def place():
    tile, tiles = lax.axis_index("tile"), lax.axis_size("tile")
    return tile % 2 == 1, jnp.logical_or(tile == 0, tile == tiles - 1)


def half_spectrum(z_high, z_low, rows_t, side):
    r = pl.ds(pl.multiple_of(side * MARGIN, MARGIN), MARGIN)
    both = dot(jnp.concatenate([z_high, z_low], 0), rows_t[r, :WIDE])
    w = both[:WIDE] + both[WIDE:] + dot(z_high, rows_t[r, WIDE:])
    return (w[:BAND] + turn(w[BAND:])) * signs((BAND, WIDE))


def analyze_kernel(mask_hbm, rows_hbm, rows_t_hbm, odd_out, rest, rows, rows_t, mask, sems):
    moves = copies([(mask_hbm, mask), (rows_hbm, rows), (rows_t_hbm, rows_t)], sems)
    for move in moves:
        move.wait()
    odd, _ = place()
    high, low = halves(mask[...])
    both = dot(rows[...], high)
    z = both[:WIDE] + both[WIDE:] + dot(rows[:WIDE], low)
    z_left, z_right = z[:, :MARGIN], z[:, MARGIN:]
    rest[...] = jnp.where(odd, z_left, z_right)
    odd_out[...] = half_spectrum(*halves(jnp.where(odd, z_right, z_left)), rows_t, jnp.where(odd, 1, 0))


def prepare_kernel(
    rest, odd_out, rows_t, index_hbm, weight_hbm, dose_hbm, table_hbm, target_hbm,
    even_out, own, mixed, target, table, index, weight, dose, sems,
):
    moves = copies(
        [
            (index_hbm, index),
            (weight_hbm, weight),
            (dose_hbm, dose),
            (table_hbm, table),
            (target_hbm, target),
        ],
        sems,
    )
    odd, _ = place()
    even = half_spectrum(*halves(rest[...]), rows_t, jnp.where(odd, 0, 1))
    even_out[...] = even
    own[...] = (even + odd_out[...]) * signs((BAND, WIDE))
    for move in moves:
        move.wait()
    for condition in range(CONDS):
        entry = index[condition]
        for k in range(KERN):
            scale = jnp.sqrt(
                jnp.full((1, WIDE), 0.5 * steepness * dose[entry] * weight[k, entry])
            ) * (1.0 / (NPAD * NPAD))
            for part in range(2):
                kernel = table[entry, k, part]
                doubled = jnp.concatenate([kernel, kernel], 1)
                mixed[condition * KERN + k, part] = doubled * scale


def join_kernel(own, odd_in, joined):
    _, alone = place()
    joined[...] = own[...] + jnp.where(alone, 0.0, odd_in[...])


def window_kernel(joined, even_in, target, mixed, rows_t, rows, resist, grad):
    spec = joined[...] + even_in[...]
    turned = turn(spec)
    stack = jnp.concatenate(
        [stacked(mixed[i, 0] * spec + mixed[i, 1] * turned) for i in range(PAIRS)], 1
    )
    high, low = halves(stack)
    first = dot(rows_t[...], jnp.concatenate([high, high], 0)) + dot(rows_t[:, :WIDE], low)
    rows_twice = jnp.concatenate([rows[:WIDE], rows[:WIDE]], 0)
    q_parts = [[] for _ in range(PAIRS)]
    for condition in range(CONDS):
        group = [condition * KERN + k for k in range(KERN)]
        for start in range(0, CORE, CHUNK):
            r = slice(start, start + CHUNK)
            y = jnp.concatenate([first[r, i * WIDE : (i + 1) * WIDE] for i in group], 0)
            y_high, y_low = halves(jnp.concatenate([y, -turn(y)], 0))
            f = dot(jnp.concatenate([y_high, y_low], 1), rows_twice) + dot(y_high, rows[WIDE:])
            squares = f * f
            power = sum(squares[i * CHUNK : (i + 1) * CHUNK] for i in range(2 * KERN))
            t = jnp.tanh(power - 0.5 * steepness * threshold)
            resist[condition, r] = 0.5 + 0.5 * t
            drive = (t + (1.0 - 2.0 * target[r])) * (2.0 - 2.0 * (t * t))
            s_high, s_low = halves(jnp.concatenate([drive] * (2 * KERN), 0) * f)
            both = dot(s_high, rows_t[...])
            u = both[:, :WIDE] + both[:, WIDE:] + dot(s_low, rows_t[:, :WIDE])
            q = u[: KERN * CHUNK] + turn(u[KERN * CHUNK :])
            for k in range(KERN):
                q_parts[group[k]].append(q[k * CHUNK : (k + 1) * CHUNK])
    q = jnp.concatenate([jnp.concatenate(p, 0) for p in q_parts], 1)
    q_high, q_low = halves(q)
    both = dot(rows[...], q_high)
    u = both[:WIDE] + both[WIDE:] + dot(rows[:WIDE], q_low)
    total = jnp.zeros((BAND, WIDE), jnp.float32)
    for i in range(PAIRS):
        c = slice(i * WIDE, (i + 1) * WIDE)
        back = u[:BAND, c] + turn(u[BAND:, c])
        total = total + mixed[i, 0] * back - mixed[i, 1] * turn(back)
    grad[...] = total


def synthesize(spec, rows, rows_t, side, out):
    high, low = halves(stacked(spec))
    y = dot(rows_t[...], jnp.concatenate([high, high], 0)) + dot(rows_t[:, :WIDE], low)
    y_high, y_low = halves(y)
    c = pl.ds(pl.multiple_of(side * MARGIN, MARGIN), MARGIN)
    both = dot(jnp.concatenate([y_high, y_low], 0), rows[:WIDE, c])
    out[...] = both[:CORE] + both[CORE:] + dot(y_high, rows[WIDE:, c])


def beside_kernel(own, even_in, rows, rows_t, resist, resist_hbm, gradient_hbm, out, sems):
    odd, _ = place()
    side = jnp.where(odd, 0, 1)
    first = copies([(resist, resist_hbm)], sems)[0]
    synthesize(own[...] + even_in[...] * signs((BAND, WIDE)), rows, rows_t, side, out)
    c = pl.ds(pl.multiple_of(side * MARGIN, MARGIN), MARGIN)
    second = pltpu.make_async_copy(out, gradient_hbm.at[:, c], sems.at[1])
    second.start()
    first.wait()
    second.wait()


def across_kernel(own, odd_in, rows, rows_t, half_hbm, gradient_hbm, out, sems):
    odd, alone = place()
    side = jnp.where(odd, 1, 0)
    extra = jnp.where(alone, 0.0, odd_in[...] * signs((BAND, WIDE)))
    synthesize(own[...] + extra, rows, rows_t, side, out)
    c = pl.ds(pl.multiple_of(side * MARGIN, MARGIN), MARGIN)
    move = pltpu.make_async_copy(out, gradient_hbm.at[:, c], sems.at[0])
    move.start()
    move.wait()


def pinned(*arrays):
    return [pltpu.with_memory_space_constraint(jnp.asarray(a), pltpu.HBM) for a in arrays]


SPACES = {"v": pltpu.VMEM, "h": pltpu.HBM, "s": pltpu.SMEM}


def call(kernel, ins, outs, scratch=(), aliases=None, flops=10**6):
    shapes = [jax.ShapeDtypeStruct(shape, dtype) for _, shape, dtype in outs]
    specs = [pl.BlockSpec(memory_space=SPACES[o[0]]) for o in outs]
    return pl.pallas_call(
        kernel,
        out_shape=shapes if len(shapes) > 1 else shapes[0],
        in_specs=[pl.BlockSpec(memory_space=SPACES[i]) for i in ins],
        out_specs=specs if len(specs) > 1 else specs[0],
        scratch_shapes=list(scratch),
        input_output_aliases=aliases or {},
        compiler_params=pltpu.CompilerParams(vmem_limit_bytes=16 << 20),
        cost_estimate=pl.CostEstimate(flops=flops, bytes_accessed=1 << 16, transcendentals=0),
    )


def partners(windows, tiles):
    even = [(w * tiles + i, w * tiles + (i ^ 1)) for w in range(windows) for i in range(tiles)]
    odd = []
    for w in range(windows):
        base = w * tiles
        for i in range(1, tiles - 1, 2):
            odd += [(base + i, base + i + 1), (base + i + 1, base + i)]
        other = w ^ 1 if (w ^ 1) < windows else w
        for i in (0, tiles - 1):
            odd.append((base + i, other * tiles + i))
    return even, odd


def local(mask, target, kernel_table, kernel_weight, dose_table, condition_index):
    rows_table = np.concatenate(parts(tables()), 0)
    rows_t_table = np.ascontiguousarray(rows_table.T)
    even, odd = partners(lax.axis_size("win"), lax.axis_size("tile"))
    over = ("win", "tile")
    f32, bf16 = jnp.float32, jnp.bfloat16
    small = ("v", (BAND, WIDE), f32)
    square = (CORE, CORE)
    dma, smem = pltpu.SemaphoreType.DMA, pltpu.SMEM
    to_odd, rest, rows, rows_t = call(
        analyze_kernel,
        "hhh",
        [small, ("v", (WIDE, MARGIN), f32)] + [("v", square, bf16)] * 2,
        [pltpu.VMEM(square, f32), dma((3,))],
    )(*pinned(mask, rows_table, rows_t_table))
    from_odd = lax.ppermute(to_odd, over, odd)
    to_even, own, mixed, goal = call(
        prepare_kernel,
        "vvvhhhhh",
        [small, small, ("v", (PAIRS, 2, BAND, WIDE), f32), ("v", square, f32)],
        [
            pltpu.VMEM((TABLE, KERN, 2, BAND, BAND), f32),
            smem((CONDS,), jnp.int32),
            smem((KERN, TABLE), f32),
            smem((TABLE,), f32),
            dma((5,)),
        ],
    )(
        rest, to_odd, rows_t,
        *pinned(condition_index, kernel_weight.T, dose_table, kernel_table, target),
    )
    from_even = lax.ppermute(to_even, over, even)
    joined = call(join_kernel, "vv", [small])(own, from_odd)
    resist, grad = call(
        window_kernel, "v" * 6, [("v", (CONDS, CORE, CORE), f32), small]
    )(joined, from_even, goal, mixed, rows_t, rows)
    from_odd = lax.ppermute(grad, over, odd)
    from_even = lax.ppermute(grad, over, even)
    strip = pltpu.VMEM((CORE, MARGIN), f32)
    resist, gradient = call(
        beside_kernel,
        "v" * 5,
        [("h", (CONDS, CORE, CORE), f32), ("h", square, f32)],
        [strip, dma((2,))],
    )(grad, from_even, rows, rows_t, resist)
    gradient = call(
        across_kernel, "vvvvh", [("h", square, f32)], [strip, dma((1,))], {4: 0}
    )(grad, from_odd, rows, rows_t, gradient)
    return (resist, gradient)


def solution(mesh):
    return jax.shard_map(
        local,
        mesh=mesh,
        in_specs=(P("win", "tile"), P("win", "tile"), P(), P(), P(), P()),
        out_specs=(P(None, "win", "tile"), P("win", "tile")),
        check_vma=False,
    )
```

```python
import math

import jax
import jax.numpy as jnp
import ml_dtypes
import numpy as np
from jax import lax
from jax.experimental import pallas as pl
from jax.experimental.pallas import tpu as pltpu
from jax.sharding import PartitionSpec as P

NPAD = 512
MARGIN = 128
BAND = 64
KERN = 2
TABLE = 4
TABLES = 7
CONDS = 2
CORE = 256
PAIRS = CONDS * KERN
WIDE = 2 * BAND
CHUNK = 128
COARSE = 2 * BAND
STEP = NPAD // COARSE

steepness = 6.0
threshold = 0.3


def parts(table):
    high = table.astype(ml_dtypes.bfloat16)
    low = (table - high.astype(np.float64)).astype(ml_dtypes.bfloat16)
    return high, low


def waves(positions):
    frequency = np.arange(BAND)[:, None] - BAND // 2
    phase = (frequency * positions[None, :] % NPAD) * (2.0 * math.pi / NPAD)
    return np.concatenate([np.cos(phase), -np.sin(phase)], 0)


def interpolation():
    apart = np.arange(MARGIN, MARGIN + CORE)[:, None] - STEP * np.arange(COARSE)[None, :]
    frequency = np.arange(1, COARSE // 2)[:, None, None]
    total = 1.0 + 2.0 * np.cos((frequency * apart % NPAD) * (2.0 * math.pi / NPAD)).sum(0)
    total = total + np.cos((COARSE // 2 * apart % NPAD) * (2.0 * math.pi / NPAD))
    return total / COARSE


def side_by_side(table):
    return np.concatenate(parts(table), 1)


def halves(x):
    high = x.astype(jnp.bfloat16)
    return high, (x - high.astype(jnp.float32)).astype(jnp.bfloat16)


def dot(a, b):
    return jnp.dot(a, b, preferred_element_type=jnp.float32)


def turn(x):
    lane = lax.broadcasted_iota(jnp.int32, x.shape, 1)
    rolled = pltpu.roll(x, BAND, 1)
    return jnp.where(lane < BAND, -rolled, rolled)


def signs(shape):
    lane = lax.broadcasted_iota(jnp.int32, shape, 1)
    return jnp.where(lane % 2 == 0, 1.0, -1.0).astype(jnp.float32)


def stacked(x):
    return jnp.concatenate([x, -turn(x)], 0)


def copies(pairs, sems):
    moves = [pltpu.make_async_copy(a, b, sems.at[i]) for i, (a, b) in enumerate(pairs)]
    for move in moves:
        move.start()
    return moves


def place():
    tile, tiles = lax.axis_index("tile"), lax.axis_size("tile")
    return tile % 2 == 1, jnp.logical_or(tile == 0, tile == tiles - 1)


def half_spectrum(z_high, z_low, rows_t, side):
    r = pl.ds(pl.multiple_of(side * MARGIN, MARGIN), MARGIN)
    both = dot(jnp.concatenate([z_high, z_low], 0), rows_t[r, :WIDE])
    w = both[:WIDE] + both[WIDE:] + dot(z_high, rows_t[r, WIDE:])
    return (w[:BAND] + turn(w[BAND:])) * signs((BAND, WIDE))


def analyze_kernel(mask_hbm, rows_hbm, rows_t_hbm, odd_out, rest, rows, rows_t, mask, sems):
    moves = copies([(mask_hbm, mask), (rows_hbm, rows), (rows_t_hbm, rows_t)], sems)
    for move in moves:
        move.wait()
    odd, _ = place()
    high, low = halves(mask[...])
    both = dot(rows[...], high)
    z = both[:WIDE] + both[WIDE:] + dot(rows[:WIDE], low)
    z_left, z_right = z[:, :MARGIN], z[:, MARGIN:]
    rest[...] = jnp.where(odd, z_left, z_right)
    odd_out[...] = half_spectrum(*halves(jnp.where(odd, z_right, z_left)), rows_t, jnp.where(odd, 1, 0))


def own_kernel(rest, odd_out, rows_t, even_out, own):
    odd, _ = place()
    even = half_spectrum(*halves(rest[...]), rows_t, jnp.where(odd, 0, 1))
    even_out[...] = even
    own[...] = (even + odd_out[...]) * signs((BAND, WIDE))


def prepare_kernel(
    after, index_hbm, weight_hbm, dose_hbm, table_hbm, target_hbm, *refs
):
    hbm, refs = refs[:TABLES], refs[TABLES:]
    mixed, goal, tables = refs[0], refs[1], refs[2 : 2 + TABLES]
    target, table, index, weight, dose, sems = refs[2 + TABLES :]
    moves = copies(
        [
            (index_hbm, index),
            (weight_hbm, weight),
            (dose_hbm, dose),
            (table_hbm, table),
            (target_hbm, target),
            *zip(hbm, tables),
        ],
        sems,
    )
    for move in moves:
        move.wait()
    for condition in range(CONDS):
        entry = index[condition]
        for k in range(KERN):
            scale = jnp.sqrt(
                jnp.full((1, WIDE), 0.5 * steepness * dose[entry] * weight[k, entry])
            ) * (1.0 / (NPAD * NPAD))
            for part in range(2):
                kernel = table[entry, k, part]
                doubled = jnp.concatenate([kernel, kernel], 1)
                mixed[condition * KERN + k, part] = doubled * scale
    goal[...] = 1.0 - 2.0 * target[...]


def join_kernel(own, odd_in, joined):
    _, alone = place()
    joined[...] = own[...] + jnp.where(alone, 0.0, odd_in[...])


def window_kernel(
    joined, even_in, goal, mixed, points, points_t, out_high, out_low, back_both, finer, finer_t,
    resist, grad,
):
    spec = joined[...] + even_in[...]
    turned = turn(spec)
    out_twice = jnp.concatenate([out_high[...], out_high[...]], 0)
    finer_twice = jnp.concatenate([finer_t[:COARSE], finer_t[:COARSE]], 0)
    conditions = range(CONDS)

    def coarse_rows(condition):
        group = range(condition * KERN, (condition + 1) * KERN)
        top = jnp.concatenate([mixed[i, 0] * spec + mixed[i, 1] * turned for i in group], 1)
        bottom = jnp.concatenate([mixed[i, 1] * spec - mixed[i, 0] * turned for i in group], 1)
        high, low = halves(jnp.concatenate([top, bottom], 0))
        return dot(points_t[...], jnp.concatenate([high, high], 0)) + dot(points_t[:, :WIDE], low)

    def coarse_field(y):
        y = jnp.concatenate([y[:, k * WIDE : (k + 1) * WIDE] for k in range(KERN)], 0)
        high, low = halves(y)
        return dot(jnp.concatenate([high, low], 1), out_twice) + dot(high, out_low[...])

    def finer_rows(f):
        squares = f * f
        power = sum(
            squares[k * COARSE : (k + 1) * COARSE, c]
            for k in range(KERN)
            for c in (slice(0, COARSE), slice(COARSE, 2 * COARSE))
        )
        high, low = halves(power - 0.5 * steepness * threshold)
        return dot(finer[...], jnp.concatenate([high, high], 0)) + dot(finer[:, :COARSE], low)

    def finer_columns(z):
        z_high, z_low = halves(z)
        return dot(jnp.concatenate([z_high, z_low], 1), finer_twice) + dot(z_high, finer_t[COARSE:])

    def print_and_drive(condition, r, power):
        t = jnp.tanh(power)
        resist[condition, r] = 0.5 + 0.5 * t
        return (t + goal[r]) * (1.0 - t * t)

    def coarser_columns(drive):
        high, low = halves(drive)
        both = dot(high, finer[...])
        return both[:, :COARSE] + both[:, COARSE:] + dot(low, finer[:, :COARSE])

    def coarser_rows(w):
        high, low = halves(w)
        both = dot(finer_t[...], high)
        return both[:COARSE] + both[COARSE:] + dot(finer_t[:COARSE], low)

    def back_columns(drive, f):
        drive = jnp.concatenate([drive, drive], 1)
        high, low = halves(jnp.concatenate([drive] * KERN, 0) * f)
        both = dot(high, back_both[...])
        q = both[:, :WIDE] + both[:, WIDE:] + dot(low, back_both[:, :WIDE])
        return jnp.concatenate([q[k * COARSE : (k + 1) * COARSE] for k in range(KERN)], 1)

    def back_rows(q):
        high, low = halves(q)
        return dot(points[...], jnp.concatenate([high, high], 0)) + dot(points[:, :COARSE], low)

    y = [coarse_rows(c) for c in conditions]
    fields = [coarse_field(x) for x in y]
    z = [finer_rows(f) for f in fields]
    pieces = [slice(start, start + CHUNK) for start in range(0, CORE, CHUNK)]
    power = [[finer_columns(z[c][r]) for c in conditions] for r in pieces]
    drive = [[print_and_drive(c, r, p[c]) for c in conditions] for r, p in zip(pieces, power)]
    w = [[coarser_columns(d[c]) for c in conditions] for d in drive]
    w = [jnp.concatenate([x[c] for x in w], 0) for c in conditions]
    drive = [coarser_rows(x) for x in w]
    q = [back_columns(drive[c], fields[c]) for c in conditions]
    u = [back_rows(x) for x in q]
    straight = jnp.zeros((BAND, WIDE), jnp.float32)
    crossed = jnp.zeros((BAND, WIDE), jnp.float32)
    for i in range(PAIRS):
        c = slice(i % KERN * WIDE, (i % KERN + 1) * WIDE)
        top, bottom = u[i // KERN][:BAND, c], u[i // KERN][BAND:, c]
        straight = straight + (mixed[i, 0] * top + mixed[i, 1] * bottom)
        crossed = crossed + (mixed[i, 0] * bottom - mixed[i, 1] * top)
    grad[...] = 2.0 * (straight + turn(crossed))


def synthesize(spec, rows, rows_t, side, out):
    high, low = halves(stacked(spec))
    y = dot(rows_t[...], jnp.concatenate([high, high], 0)) + dot(rows_t[:, :WIDE], low)
    y_high, y_low = halves(y)
    c = pl.ds(pl.multiple_of(side * MARGIN, MARGIN), MARGIN)
    both = dot(jnp.concatenate([y_high, y_low], 0), rows[:WIDE, c])
    out[...] = both[:CORE] + both[CORE:] + dot(y_high, rows[WIDE:, c])


def beside_kernel(own, even_in, rows, rows_t, resist, resist_hbm, gradient_hbm, out, sems):
    odd, _ = place()
    side = jnp.where(odd, 0, 1)
    first = copies([(resist, resist_hbm)], sems)[0]
    synthesize(own[...] + even_in[...] * signs((BAND, WIDE)), rows, rows_t, side, out)
    c = pl.ds(pl.multiple_of(side * MARGIN, MARGIN), MARGIN)
    second = pltpu.make_async_copy(out, gradient_hbm.at[:, c], sems.at[1])
    second.start()
    first.wait()
    second.wait()


def across_kernel(own, odd_in, rows, rows_t, half_hbm, gradient_hbm, out, sems):
    odd, alone = place()
    side = jnp.where(odd, 1, 0)
    extra = jnp.where(alone, 0.0, odd_in[...] * signs((BAND, WIDE)))
    synthesize(own[...] + extra, rows, rows_t, side, out)
    c = pl.ds(pl.multiple_of(side * MARGIN, MARGIN), MARGIN)
    move = pltpu.make_async_copy(out, gradient_hbm.at[:, c], sems.at[0])
    move.start()
    move.wait()


def pinned(*arrays):
    return [pltpu.with_memory_space_constraint(jnp.asarray(a), pltpu.HBM) for a in arrays]


SPACES = {"v": pltpu.VMEM, "h": pltpu.HBM, "s": pltpu.SMEM}


def call(kernel, ins, outs, scratch=(), aliases=None, flops=10**6):
    shapes = [jax.ShapeDtypeStruct(shape, dtype) for _, shape, dtype in outs]
    specs = [pl.BlockSpec(memory_space=SPACES[o[0]]) for o in outs]
    return pl.pallas_call(
        kernel,
        out_shape=shapes if len(shapes) > 1 else shapes[0],
        in_specs=[pl.BlockSpec(memory_space=SPACES[i]) for i in ins],
        out_specs=specs if len(specs) > 1 else specs[0],
        scratch_shapes=list(scratch),
        input_output_aliases=aliases or {},
        compiler_params=pltpu.CompilerParams(vmem_limit_bytes=16 << 20),
        cost_estimate=pl.CostEstimate(flops=flops, bytes_accessed=1 << 16, transcendentals=0),
    )


def partners(windows, tiles):
    even = [(w * tiles + i, w * tiles + (i ^ 1)) for w in range(windows) for i in range(tiles)]
    odd = []
    for w in range(windows):
        base = w * tiles
        for i in range(1, tiles - 1, 2):
            odd += [(base + i, base + i + 1), (base + i + 1, base + i)]
        other = w ^ 1 if (w ^ 1) < windows else w
        for i in (0, tiles - 1):
            odd.append((base + i, other * tiles + i))
    return even, odd


def local(mask, target, kernel_table, kernel_weight, dose_table, condition_index):
    rows_table = np.concatenate(parts(waves(np.arange(MARGIN, MARGIN + CORE))), 0)
    rows_t_table = np.ascontiguousarray(rows_table.T)
    points = waves(STEP * np.arange(COARSE))
    cosine, sine = points[:BAND], points[BAND:]
    out = np.block([[cosine, -sine], [sine, cosine]])
    back = np.block([[cosine.T, sine.T], [-sine.T, cosine.T]])
    finer = side_by_side(interpolation())
    coarse_tables = (
        side_by_side(points), side_by_side(points.T), *parts(out), side_by_side(back),
        finer, np.ascontiguousarray(finer.T),
    )
    even, odd = partners(lax.axis_size("win"), lax.axis_size("tile"))
    over = ("win", "tile")
    f32, bf16 = jnp.float32, jnp.bfloat16
    small = ("v", (BAND, WIDE), f32)
    square = (CORE, CORE)
    dma, smem = pltpu.SemaphoreType.DMA, pltpu.SMEM
    to_odd, rest, rows, rows_t = call(
        analyze_kernel,
        "hhh",
        [small, ("v", (WIDE, MARGIN), f32)] + [("v", square, bf16)] * 2,
        [pltpu.VMEM(square, f32), dma((3,))],
    )(*pinned(mask, rows_table, rows_t_table))
    from_odd = lax.ppermute(to_odd, over, odd)
    to_even, own = call(own_kernel, "vvv", [small, small])(rest, to_odd, rows_t)
    from_even = lax.ppermute(to_even, over, even)
    mixed, goal, *coarse = call(
        prepare_kernel,
        "v" + "h" * (5 + TABLES),
        [("v", (PAIRS, 2, BAND, WIDE), f32), ("v", square, f32)]
        + [("v", table.shape, bf16) for table in coarse_tables],
        [
            pltpu.VMEM(square, f32),
            pltpu.VMEM((TABLE, KERN, 2, BAND, BAND), f32),
            smem((CONDS,), jnp.int32),
            smem((KERN, TABLE), f32),
            smem((TABLE,), f32),
            dma((5 + TABLES,)),
        ],
    )(
        own,
        *pinned(condition_index, kernel_weight.T, dose_table, kernel_table, target, *coarse_tables),
    )
    joined = call(join_kernel, "vv", [small])(own, from_odd)
    resist, grad = call(
        window_kernel, "v" * (4 + TABLES), [("v", (CONDS, CORE, CORE), f32), small]
    )(joined, from_even, goal, mixed, *coarse)
    from_odd = lax.ppermute(grad, over, odd)
    from_even = lax.ppermute(grad, over, even)
    strip = pltpu.VMEM((CORE, MARGIN), f32)
    resist, gradient = call(
        beside_kernel,
        "v" * 5,
        [("h", (CONDS, CORE, CORE), f32), ("h", square, f32)],
        [strip, dma((2,))],
    )(grad, from_even, rows, rows_t, resist)
    gradient = call(
        across_kernel, "vvvvh", [("h", square, f32)], [strip, dma((1,))], {4: 0}
    )(grad, from_odd, rows, rows_t, gradient)
    return (resist, gradient)


def solution(mesh):
    return jax.shard_map(
        local,
        mesh=mesh,
        in_specs=(P("win", "tile"), P("win", "tile"), P(), P(), P(), P()),
        out_specs=(P(None, "win", "tile"), P("win", "tile")),
        check_vma=False,
    )
```

```python
import math

import jax
import jax.numpy as jnp
import ml_dtypes
import numpy as np
from jax import lax
from jax.experimental import pallas as pl
from jax.experimental.pallas import tpu as pltpu
from jax.sharding import PartitionSpec as P

NPAD = 512
MARGIN = 128
BAND = 64
KERN = 2
TABLE = 4
TSPLIT = 2
CSPLIT = 3
CONDS = 2
CORE = 256
PAIRS = CONDS * KERN
WIDE = 2 * BAND
CHUNK = 256
COARSE = 2 * BAND
STEP = NPAD // COARSE

steepness = 6.0
threshold = 0.3


def parts(table):
    high = table.astype(ml_dtypes.bfloat16)
    low = (table - high.astype(np.float64)).astype(ml_dtypes.bfloat16)
    return high, low


def waves(positions):
    frequency = np.arange(BAND)[:, None] - BAND // 2
    phase = (frequency * positions[None, :] % NPAD) * (2.0 * math.pi / NPAD)
    return np.concatenate([np.cos(phase), -np.sin(phase)], 0)


def interpolation():
    apart = np.arange(MARGIN, MARGIN + CORE)[:, None] - STEP * np.arange(COARSE)[None, :]
    frequency = np.arange(1, COARSE // 2)[:, None, None]
    total = 1.0 + 2.0 * np.cos((frequency * apart % NPAD) * (2.0 * math.pi / NPAD)).sum(0)
    total = total + np.cos((COARSE // 2 * apart % NPAD) * (2.0 * math.pi / NPAD))
    return total / COARSE


def side_by_side(table):
    return np.concatenate(parts(table), 1)


def later_tables(rows_table):
    points = waves(STEP * np.arange(COARSE))
    cosine, sine = points[:BAND], points[BAND:]
    out = np.block([[cosine, -sine], [sine, cosine]])
    back = np.block([[cosine.T, sine.T], [-sine.T, cosine.T]])
    finer = side_by_side(interpolation())
    return np.concatenate(
        [side_by_side(points), side_by_side(points.T), *parts(out), side_by_side(back), finer, finer.T, rows_table.T]
    )


def table_parts(tables):
    ends = np.cumsum([WIDE, COARSE, WIDE, WIDE, 2 * COARSE, CORE, CORE, CORE])
    return [tables.at[int(end - size) : int(end)] for end, size in zip(ends, np.diff(ends, prepend=0))]


def halves(x):
    high = x.astype(jnp.bfloat16)
    return high, (x - high.astype(jnp.float32)).astype(jnp.bfloat16)


def dot(a, b):
    return jnp.dot(a, b, preferred_element_type=jnp.float32)


def turn(x):
    lane = lax.broadcasted_iota(jnp.int32, x.shape, 1)
    rolled = pltpu.roll(x, BAND, 1)
    return jnp.where(lane < BAND, -rolled, rolled)


def signs(shape):
    lane = lax.broadcasted_iota(jnp.int32, shape, 1)
    return jnp.where(lane % 2 == 0, 1.0, -1.0).astype(jnp.float32)


def stacked(x):
    return jnp.concatenate([x, -turn(x)], 0)


def strips(source, target, rows):
    return [
        (source.at[start : start + rows], target.at[start : start + rows])
        for start in range(0, source.shape[0], rows)
    ]


def copies(pairs, sems):
    moves = [pltpu.make_async_copy(a, b, sems.at[i]) for i, (a, b) in enumerate(pairs)]
    for move in moves:
        move.start()
    return moves


def place():
    tile, tiles = lax.axis_index("tile"), lax.axis_size("tile")
    return tile % 2 == 1, jnp.logical_or(tile == 0, tile == tiles - 1)


def across_lanes(a, b):
    return lax.dot_general(a, b, (((1,), (1,)), ((), ())), preferred_element_type=jnp.float32)


def half_spectrum(z, rows, side):
    columns = rows[:, pl.ds(pl.multiple_of(side * MARGIN, MARGIN), MARGIN)]
    both = across_lanes(
        jnp.concatenate(halves(z), 1), jnp.concatenate([columns, columns], 1)
    )
    w = both[:, :WIDE] + both[:, WIDE:]
    return (w[:BAND] + turn(w[BAND:])) * signs((BAND, WIDE))


def analyze_kernel(mask_hbm, rows_hbm, odd_out, rest, rows, mask, sems):
    for move in copies([(mask_hbm, mask), (rows_hbm, rows)], sems):
        move.wait()
    odd, _ = place()
    high, low = halves(mask[...])
    both = dot(rows[...], high)
    z = both[:WIDE] + both[WIDE:] + dot(rows[:WIDE], low)
    z_left, z_right = z[:, :MARGIN], z[:, MARGIN:]
    rest[...] = jnp.where(odd, z_left, z_right)
    odd_out[...] = half_spectrum(jnp.where(odd, z_right, z_left), rows, jnp.where(odd, 1, 0))


def own_kernel(rest, odd_out, rows, even_out, own):
    odd, _ = place()
    even = half_spectrum(rest[...], rows, jnp.where(odd, 0, 1))
    even_out[...] = even
    own[...] = (even + odd_out[...]) * signs((BAND, WIDE))


def prepare_kernel(
    after, index_hbm, weight_hbm, dose_hbm, table_hbm, target_hbm, tables_hbm,
    mixed, goal, tables, target, table, index, weight, dose, sems,
):
    moves = copies(
        [
            (index_hbm, index),
            (weight_hbm, weight),
            (dose_hbm, dose),
            *strips(table_hbm, table, TABLE // TSPLIT),
            (target_hbm, target),
            *strips(tables_hbm, tables, tables.shape[0] // CSPLIT),
        ],
        sems,
    )
    for move in moves:
        move.wait()
    for condition in range(CONDS):
        entry = index[condition]
        for k in range(KERN):
            scale = jnp.sqrt(
                jnp.full((1, WIDE), 0.5 * steepness * dose[entry] * weight[k, entry])
            ) * (1.0 / (NPAD * NPAD))
            for part in range(2):
                kernel = table[entry, k, part]
                doubled = jnp.concatenate([kernel, kernel], 1)
                mixed[condition * KERN + k, part] = doubled * scale
    goal[...] = 1.0 - 2.0 * target[...]


def join_kernel(own, odd_in, joined):
    _, alone = place()
    joined[...] = own[...] + jnp.where(alone, 0.0, odd_in[...])


def window_kernel(joined, even_in, goal, mixed, tables, resist, grad):
    points, points_t, out_high, out_low, back_both, finer, finer_t, _ = table_parts(tables)
    spec = joined[...] + even_in[...]
    turned = turn(spec)
    out_twice = jnp.concatenate([out_high[...], out_high[...]], 0)
    finer_twice = jnp.concatenate([finer_t[:COARSE], finer_t[:COARSE]], 0)
    conditions = range(CONDS)

    def coarse_rows(condition):
        group = range(condition * KERN, (condition + 1) * KERN)
        top = jnp.concatenate([mixed[i, 0] * spec + mixed[i, 1] * turned for i in group], 1)
        bottom = jnp.concatenate([mixed[i, 1] * spec - mixed[i, 0] * turned for i in group], 1)
        high, low = halves(jnp.concatenate([top, bottom], 0))
        return dot(points_t[...], jnp.concatenate([high, high], 0)) + dot(points_t[:, :WIDE], low)

    def coarse_field(y):
        y = jnp.concatenate([y[:, k * WIDE : (k + 1) * WIDE] for k in range(KERN)], 0)
        high, low = halves(y)
        return dot(jnp.concatenate([high, low], 1), out_twice) + dot(high, out_low[...])

    def finer_rows(f):
        squares = f * f
        power = sum(
            squares[k * COARSE : (k + 1) * COARSE, c]
            for k in range(KERN)
            for c in (slice(0, COARSE), slice(COARSE, 2 * COARSE))
        )
        high, low = halves(power - 0.5 * steepness * threshold)
        both = jnp.concatenate([high, low], 1)
        both = dot(finer[...], jnp.concatenate([both, both], 0))
        return both[:, :COARSE] + both[:, COARSE:]

    def finer_columns(z):
        z_high, z_low = halves(z)
        return dot(jnp.concatenate([z_high, z_low], 1), finer_twice) + dot(z_high, finer_t[COARSE:])

    def print_and_drive(condition, r, power):
        t = jnp.tanh(power)
        resist[condition, r] = 0.5 + 0.5 * t
        return (t + goal[r]) * (1.0 - t * t)

    def coarser_columns(drive):
        high, low = halves(drive)
        both = dot(high, finer[...])
        return both[:, :COARSE] + both[:, COARSE:] + dot(low, finer[:, :COARSE])

    def coarser_rows(w):
        high, low = halves(w)
        both = dot(finer_t[:COARSE], jnp.concatenate([high, low], 1))
        return both[:, :COARSE] + both[:, COARSE:] + dot(finer_t[COARSE:], high)

    def back_columns(drive, f):
        drive = jnp.concatenate([drive, drive], 1)
        high, low = halves(jnp.concatenate([drive] * KERN, 0) * f)
        both = dot(high, back_both[...])
        q = both[:, :WIDE] + both[:, WIDE:] + dot(low, back_both[:, :WIDE])
        return jnp.concatenate([q[k * COARSE : (k + 1) * COARSE] for k in range(KERN)], 1)

    def back_rows(q):
        high, low = halves(q)
        return dot(points[...], jnp.concatenate([high, high], 0)) + dot(points[:, :COARSE], low)

    y = [coarse_rows(c) for c in conditions]
    fields = [coarse_field(x) for x in y]
    z = [finer_rows(f) for f in fields]
    pieces = [slice(start, start + CHUNK) for start in range(0, CORE, CHUNK)]
    power = [[finer_columns(z[c][r]) for c in conditions] for r in pieces]
    drive = [[print_and_drive(c, r, p[c]) for c in conditions] for r, p in zip(pieces, power)]
    w = [[coarser_columns(d[c]) for c in conditions] for d in drive]
    w = [jnp.concatenate([x[c] for x in w], 0) for c in conditions]
    drive = [coarser_rows(x) for x in w]
    q = [back_columns(drive[c], fields[c]) for c in conditions]
    u = [back_rows(x) for x in q]
    straight = jnp.zeros((BAND, WIDE), jnp.float32)
    crossed = jnp.zeros((BAND, WIDE), jnp.float32)
    for i in range(PAIRS):
        c = slice(i % KERN * WIDE, (i % KERN + 1) * WIDE)
        top, bottom = u[i // KERN][:BAND, c], u[i // KERN][BAND:, c]
        straight = straight + (mixed[i, 0] * top + mixed[i, 1] * bottom)
        crossed = crossed + (mixed[i, 0] * bottom - mixed[i, 1] * top)
    grad[...] = 2.0 * (straight + turn(crossed))


def synthesize(spec, rows, rows_t, side, out):
    both = jnp.concatenate(halves(stacked(spec)), 1)
    y = dot(rows_t[...], jnp.concatenate([both, both], 0))
    y = jnp.concatenate(halves(y[:, :WIDE] + y[:, WIDE:]), 1)
    c = pl.ds(pl.multiple_of(side * MARGIN, MARGIN), MARGIN)
    columns = jnp.concatenate([rows[:WIDE, c], rows[WIDE:, c]], 1)
    both = dot(y, jnp.concatenate([columns, columns], 0))
    out[...] = both[:, :MARGIN] + both[:, MARGIN:]


def beside_kernel(own, even_in, rows, tables, resist, resist_hbm, gradient_hbm, out, sems):
    rows_t = table_parts(tables)[-1]
    odd, _ = place()
    side = jnp.where(odd, 0, 1)
    first = copies([(resist, resist_hbm)], sems)[0]
    synthesize(own[...] + even_in[...] * signs((BAND, WIDE)), rows, rows_t, side, out)
    c = pl.ds(pl.multiple_of(side * MARGIN, MARGIN), MARGIN)
    second = pltpu.make_async_copy(out, gradient_hbm.at[:, c], sems.at[1])
    second.start()
    first.wait()
    second.wait()


def across_kernel(own, odd_in, rows, tables, half_hbm, gradient_hbm, out, sems):
    rows_t = table_parts(tables)[-1]
    odd, alone = place()
    side = jnp.where(odd, 1, 0)
    extra = jnp.where(alone, 0.0, odd_in[...] * signs((BAND, WIDE)))
    synthesize(own[...] + extra, rows, rows_t, side, out)
    c = pl.ds(pl.multiple_of(side * MARGIN, MARGIN), MARGIN)
    move = pltpu.make_async_copy(out, gradient_hbm.at[:, c], sems.at[0])
    move.start()
    move.wait()


def pinned(*arrays):
    return [pltpu.with_memory_space_constraint(jnp.asarray(a), pltpu.HBM) for a in arrays]


SPACES = {"v": pltpu.VMEM, "h": pltpu.HBM, "s": pltpu.SMEM}


def call(kernel, ins, outs, scratch=(), aliases=None, flops=10**6):
    shapes = [jax.ShapeDtypeStruct(shape, dtype) for _, shape, dtype in outs]
    specs = [pl.BlockSpec(memory_space=SPACES[o[0]]) for o in outs]
    return pl.pallas_call(
        kernel,
        out_shape=shapes if len(shapes) > 1 else shapes[0],
        in_specs=[pl.BlockSpec(memory_space=SPACES[i]) for i in ins],
        out_specs=specs if len(specs) > 1 else specs[0],
        scratch_shapes=list(scratch),
        input_output_aliases=aliases or {},
        compiler_params=pltpu.CompilerParams(vmem_limit_bytes=16 << 20),
        cost_estimate=pl.CostEstimate(flops=flops, bytes_accessed=1 << 16, transcendentals=0),
    )


def partners(windows, tiles):
    even = [(w * tiles + i, w * tiles + (i ^ 1)) for w in range(windows) for i in range(tiles)]
    odd = []
    for w in range(windows):
        base = w * tiles
        for i in range(1, tiles - 1, 2):
            odd += [(base + i, base + i + 1), (base + i + 1, base + i)]
        other = w ^ 1 if (w ^ 1) < windows else w
        for i in (0, tiles - 1):
            odd.append((base + i, other * tiles + i))
    return even, odd


def local(mask, target, kernel_table, kernel_weight, dose_table, condition_index):
    rows_table = np.concatenate(parts(waves(np.arange(MARGIN, MARGIN + CORE))), 0)
    tables = later_tables(rows_table)
    even, odd = partners(lax.axis_size("win"), lax.axis_size("tile"))
    over = ("win", "tile")
    f32, bf16 = jnp.float32, jnp.bfloat16
    small = ("v", (BAND, WIDE), f32)
    square = (CORE, CORE)
    dma, smem = pltpu.SemaphoreType.DMA, pltpu.SMEM
    to_odd, rest, rows = call(
        analyze_kernel,
        "hh",
        [small, ("v", (WIDE, MARGIN), f32), ("v", square, bf16)],
        [pltpu.VMEM(square, f32), dma((2,))],
    )(*pinned(mask, rows_table))
    from_odd = lax.ppermute(to_odd, over, odd)
    to_even, own = call(own_kernel, "vvv", [small, small])(rest, to_odd, rows)
    from_even = lax.ppermute(to_even, over, even)
    mixed, goal, tables = call(
        prepare_kernel,
        "v" + "h" * 6,
        [("v", (PAIRS, 2, BAND, WIDE), f32), ("v", square, f32), ("v", tables.shape, bf16)],
        [
            pltpu.VMEM(square, f32),
            pltpu.VMEM((TABLE, KERN, 2, BAND, BAND), f32),
            smem((CONDS,), jnp.int32),
            smem((KERN, TABLE), f32),
            smem((TABLE,), f32),
            dma((4 + TSPLIT + CSPLIT,)),
        ],
    )(
        own,
        *pinned(condition_index, kernel_weight.T, dose_table, kernel_table, target, tables),
    )
    joined = call(join_kernel, "vv", [small])(own, from_odd)
    resist, grad = call(
        window_kernel, "v" * 5, [("v", (CONDS, CORE, CORE), f32), small]
    )(joined, from_even, goal, mixed, tables)
    from_odd = lax.ppermute(grad, over, odd)
    from_even = lax.ppermute(grad, over, even)
    strip = pltpu.VMEM((CORE, MARGIN), f32)
    resist, gradient = call(
        beside_kernel,
        "v" * 5,
        [("h", (CONDS, CORE, CORE), f32), ("h", square, f32)],
        [strip, dma((2,))],
    )(grad, from_even, rows, tables, resist)
    gradient = call(
        across_kernel, "vvvvh", [("h", square, f32)], [strip, dma((1,))], {4: 0}
    )(grad, from_odd, rows, tables, gradient)
    return (resist, gradient)


def solution(mesh):
    return jax.shard_map(
        local,
        mesh=mesh,
        in_specs=(P("win", "tile"), P("win", "tile"), P(), P(), P(), P()),
        out_specs=(P(None, "win", "tile"), P("win", "tile")),
        check_vma=False,
    )
```

```python
import math

import jax
import jax.numpy as jnp
import ml_dtypes
import numpy as np
from jax import lax
from jax.experimental import pallas as pl
from jax.experimental.pallas import tpu as pltpu
from jax.sharding import PartitionSpec as P

NPAD = 512
MARGIN = 128
BAND = 64
KERN = 2
TABLE = 4
TSPLIT = 2
CSPLIT = 3
CONDS = 2
CORE = 256
PAIRS = CONDS * KERN
WIDE = 2 * BAND
COARSE = 2 * BAND
STEP = NPAD // COARSE

steepness = 6.0
threshold = 0.3


def parts(table):
    high = table.astype(ml_dtypes.bfloat16)
    low = (table - high.astype(np.float64)).astype(ml_dtypes.bfloat16)
    return high, low


def waves(positions):
    frequency = np.arange(BAND)[:, None] - BAND // 2
    phase = (frequency * positions[None, :] % NPAD) * (2.0 * math.pi / NPAD)
    return np.concatenate([np.cos(phase), -np.sin(phase)], 0)


def interpolation():
    apart = np.arange(MARGIN, MARGIN + CORE)[:, None] - STEP * np.arange(COARSE)[None, :]
    frequency = np.arange(1, COARSE // 2)[:, None, None]
    total = 1.0 + 2.0 * np.cos((frequency * apart % NPAD) * (2.0 * math.pi / NPAD)).sum(0)
    total = total + np.cos((COARSE // 2 * apart % NPAD) * (2.0 * math.pi / NPAD))
    return total / COARSE


def side_by_side(table):
    return np.concatenate(parts(table), 1)


def later_tables(rows_table):
    points = waves(STEP * np.arange(COARSE))
    core = waves(np.arange(MARGIN, MARGIN + CORE))
    turned = np.concatenate([-core[BAND:], core[:BAND]], 0)
    finer = side_by_side(interpolation())
    return np.concatenate(
        [
            side_by_side(points), side_by_side(points.T), *parts(turned),
            finer, finer.T, rows_table.T, side_by_side(turned.T),
        ]
    )


def table_parts(tables):
    ends = np.cumsum([WIDE, COARSE, WIDE, WIDE, CORE, CORE, 2 * CORE])
    return [tables.at[int(end - size) : int(end)] for end, size in zip(ends, np.diff(ends, prepend=0))]


def halves(x):
    high = x.astype(jnp.bfloat16)
    return high, (x - high.astype(jnp.float32)).astype(jnp.bfloat16)


def dot(a, b):
    return jnp.dot(a, b, preferred_element_type=jnp.float32)


def turn(x):
    lane = lax.broadcasted_iota(jnp.int32, x.shape, 1)
    rolled = pltpu.roll(x, BAND, 1)
    return jnp.where(lane < BAND, -rolled, rolled)


def signs(shape):
    lane = lax.broadcasted_iota(jnp.int32, shape, 1)
    return jnp.where(lane % 2 == 0, 1.0, -1.0).astype(jnp.float32)


def stacked(x):
    return jnp.concatenate([x, -turn(x)], 0)


def strips(source, target, rows):
    return [
        (source.at[start : start + rows], target.at[start : start + rows])
        for start in range(0, source.shape[0], rows)
    ]


def copies(pairs, sems):
    moves = [pltpu.make_async_copy(a, b, sems.at[i]) for i, (a, b) in enumerate(pairs)]
    for move in moves:
        move.start()
    return moves


def place():
    tile, tiles = lax.axis_index("tile"), lax.axis_size("tile")
    return tile % 2 == 1, jnp.logical_or(tile == 0, tile == tiles - 1)


def across_lanes(a, b):
    return lax.dot_general(a, b, (((1,), (1,)), ((), ())), preferred_element_type=jnp.float32)


def half_spectrum(z, rows, side):
    columns = rows[:, pl.ds(pl.multiple_of(side * MARGIN, MARGIN), MARGIN)]
    both = across_lanes(
        jnp.concatenate(halves(z), 1), jnp.concatenate([columns, columns], 1)
    )
    w = both[:, :WIDE] + both[:, WIDE:]
    return (w[:BAND] + turn(w[BAND:])) * signs((BAND, WIDE))


def analyze_kernel(mask_hbm, rows_hbm, odd_out, rest, rows, mask, sems):
    for move in copies([(mask_hbm, mask), (rows_hbm, rows)], sems):
        move.wait()
    odd, _ = place()
    high, low = halves(mask[...])
    both = dot(rows[...], high)
    z = both[:WIDE] + both[WIDE:] + dot(rows[:WIDE], low)
    z_left, z_right = z[:, :MARGIN], z[:, MARGIN:]
    rest[...] = jnp.where(odd, z_left, z_right)
    odd_out[...] = half_spectrum(jnp.where(odd, z_right, z_left), rows, jnp.where(odd, 1, 0))


def own_kernel(rest, odd_out, rows, even_out, own):
    odd, _ = place()
    even = half_spectrum(rest[...], rows, jnp.where(odd, 0, 1))
    even_out[...] = even
    own[...] = (even + odd_out[...]) * signs((BAND, WIDE))


def prepare_kernel(
    after, index_hbm, weight_hbm, dose_hbm, table_hbm, target_hbm, tables_hbm,
    mixed, goal, tables, target, table, index, weight, dose, sems,
):
    moves = copies(
        [
            (index_hbm, index),
            (weight_hbm, weight),
            (dose_hbm, dose),
            *strips(table_hbm, table, TABLE // TSPLIT),
            (target_hbm, target),
            *strips(tables_hbm, tables, tables.shape[0] // CSPLIT),
        ],
        sems,
    )
    for move in moves:
        move.wait()
    for condition in range(CONDS):
        entry = index[condition]
        for k in range(KERN):
            scale = jnp.sqrt(
                jnp.full((1, WIDE), 0.5 * steepness * dose[entry] * weight[k, entry])
            ) * (1.0 / (NPAD * NPAD))
            for part in range(2):
                kernel = table[entry, k, part]
                doubled = jnp.concatenate([kernel, kernel], 1)
                mixed[condition * KERN + k, part] = doubled * scale
    goal[...] = 1.0 - 2.0 * target[...]


def join_kernel(own, odd_in, joined):
    _, alone = place()
    joined[...] = own[...] + jnp.where(alone, 0.0, odd_in[...])


def window_kernel(joined, even_in, goal, mixed, rows, tables, resist, grad, odd_out):
    points, points_t, turned_high, turned_low, finer, finer_t, back_both = table_parts(tables)
    spec = joined[...] + even_in[...]
    turned = turn(spec)
    out_high = jnp.concatenate([rows[:WIDE], turned_high[...]], 1)
    out_low = jnp.concatenate([rows[WIDE:], turned_low[...]], 1)
    out_twice = jnp.concatenate([out_high, out_high], 0)
    conditions = range(CONDS)

    def coarse_rows(condition):
        group = range(condition * KERN, (condition + 1) * KERN)
        top = jnp.concatenate([mixed[i, 0] * spec + mixed[i, 1] * turned for i in group], 1)
        bottom = jnp.concatenate([mixed[i, 1] * spec - mixed[i, 0] * turned for i in group], 1)
        high, low = halves(jnp.concatenate([top, bottom], 0))
        return dot(points_t[...], jnp.concatenate([high, high], 0)) + dot(points_t[:, :WIDE], low)

    def coarse_field(y):
        y = jnp.concatenate([y[:, k * WIDE : (k + 1) * WIDE] for k in range(KERN)], 0)
        high, low = halves(y)
        return dot(jnp.concatenate([high, low], 1), out_twice) + dot(high, out_low)

    def finer_rows(f):
        squares = f * f
        power = sum(
            squares[k * COARSE : (k + 1) * COARSE, c]
            for k in range(KERN)
            for c in (slice(0, CORE), slice(CORE, 2 * CORE))
        )
        high, low = halves(power - 0.5 * steepness * threshold)
        both = jnp.concatenate([high, low], 1)
        both = dot(finer[...], jnp.concatenate([both, both], 0))
        return both[:, :CORE] + both[:, CORE:]

    def print_and_drive(condition, power):
        t = jnp.tanh(power)
        resist[condition] = 0.5 + 0.5 * t
        return (t + goal[...]) * (1.0 - t * t)

    def coarser_rows(drive):
        high, low = halves(drive)
        both = dot(finer_t[:COARSE], jnp.concatenate([high, low], 1))
        return both[:, :CORE] + both[:, CORE:] + dot(finer_t[COARSE:], high)

    def back_columns(drive, f):
        drive = jnp.concatenate([drive, drive], 1)
        high, low = halves(jnp.concatenate([drive] * KERN, 0) * f)
        both = dot(high, back_both[...])
        q = both[:, :WIDE] + both[:, WIDE:] + dot(low, back_both[:, :WIDE])
        return jnp.concatenate([q[k * COARSE : (k + 1) * COARSE] for k in range(KERN)], 1)

    def back_rows(q):
        high, low = halves(q)
        return dot(points[...], jnp.concatenate([high, high], 0)) + dot(points[:, :COARSE], low)

    y = [coarse_rows(c) for c in conditions]
    fields = [coarse_field(x) for x in y]
    power = [finer_rows(f) for f in fields]
    drive = [print_and_drive(c, power[c]) for c in conditions]
    drive = [coarser_rows(x) for x in drive]
    q = [back_columns(drive[c], fields[c]) for c in conditions]
    u = [back_rows(x) for x in q]
    straight = jnp.zeros((BAND, WIDE), jnp.float32)
    crossed = jnp.zeros((BAND, WIDE), jnp.float32)
    for i in range(PAIRS):
        c = slice(i % KERN * WIDE, (i % KERN + 1) * WIDE)
        top, bottom = u[i // KERN][:BAND, c], u[i // KERN][BAND:, c]
        straight = straight + (mixed[i, 0] * top + mixed[i, 1] * bottom)
        crossed = crossed + (mixed[i, 0] * bottom - mixed[i, 1] * top)
    total = 2.0 * (straight + turn(crossed))
    grad[...] = total
    odd_out[:BAND] = total
    odd_out[BAND:] = total[: odd_out.shape[0] - BAND]


def synthesize(spec, rows, rows_t, side, out):
    both = jnp.concatenate(halves(stacked(spec)), 1)
    y = dot(rows_t[...], jnp.concatenate([both, both], 0))
    y = jnp.concatenate(halves(y[:, :WIDE] + y[:, WIDE:]), 1)
    c = pl.ds(pl.multiple_of(side * MARGIN, MARGIN), MARGIN)
    columns = jnp.concatenate([rows[:WIDE, c], rows[WIDE:, c]], 1)
    both = dot(y, jnp.concatenate([columns, columns], 0))
    out[...] = both[:, :MARGIN] + both[:, MARGIN:]


def store_kernel(resist, resist_hbm, sems):
    for move in copies([(resist, resist_hbm)], sems):
        move.wait()


def beside_kernel(own, even_in, rows, tables, half):
    odd, _ = place()
    spec = own[...] + even_in[...] * signs((BAND, WIDE))
    synthesize(spec, rows, table_parts(tables)[-1].at[:CORE], jnp.where(odd, 0, 1), half)


def across_kernel(own, odd_in, rows, tables, half, gradient_hbm, out, sems):
    odd, alone = place()
    side = jnp.where(odd, 1, 0)

    def columns(side):
        return gradient_hbm.at[:, pl.ds(pl.multiple_of(side * MARGIN, MARGIN), MARGIN)]

    moves = copies([(half, columns(1 - side))], sems)
    extra = jnp.where(alone, 0.0, odd_in[:BAND] * signs((BAND, WIDE)))
    synthesize(own[...] + extra, rows, table_parts(tables)[-1].at[:CORE], side, out)
    moves += copies([(out, columns(side))], sems.at[1:])
    for move in moves:
        move.wait()


def pinned(*arrays):
    return [pltpu.with_memory_space_constraint(jnp.asarray(a), pltpu.HBM) for a in arrays]


SPACES = {"v": pltpu.VMEM, "h": pltpu.HBM, "s": pltpu.SMEM}


def call(kernel, ins, outs, scratch=(), aliases=None, flops=10**6):
    shapes = [jax.ShapeDtypeStruct(shape, dtype) for _, shape, dtype in outs]
    specs = [pl.BlockSpec(memory_space=SPACES[o[0]]) for o in outs]
    return pl.pallas_call(
        kernel,
        out_shape=shapes if len(shapes) > 1 else shapes[0],
        in_specs=[pl.BlockSpec(memory_space=SPACES[i]) for i in ins],
        out_specs=specs if len(specs) > 1 else specs[0],
        scratch_shapes=list(scratch),
        input_output_aliases=aliases or {},
        compiler_params=pltpu.CompilerParams(vmem_limit_bytes=16 << 20),
        cost_estimate=pl.CostEstimate(flops=flops, bytes_accessed=1 << 16, transcendentals=0),
    )


def partners(windows, tiles):
    even = [(w * tiles + i, w * tiles + (i ^ 1)) for w in range(windows) for i in range(tiles)]
    odd = []
    for w in range(windows):
        base = w * tiles
        for i in range(1, tiles - 1, 2):
            odd += [(base + i, base + i + 1), (base + i + 1, base + i)]
        other = w ^ 1 if (w ^ 1) < windows else w
        for i in (0, tiles - 1):
            odd.append((base + i, other * tiles + i))
    return even, odd


def local(mask, target, kernel_table, kernel_weight, dose_table, condition_index):
    rows_table = np.concatenate(parts(waves(np.arange(MARGIN, MARGIN + CORE))), 0)
    tables = later_tables(rows_table)
    even, odd = partners(lax.axis_size("win"), lax.axis_size("tile"))
    over = ("win", "tile")
    f32, bf16 = jnp.float32, jnp.bfloat16
    small = ("v", (BAND, WIDE), f32)
    square = (CORE, CORE)
    dma, smem = pltpu.SemaphoreType.DMA, pltpu.SMEM
    to_odd, rest, rows = call(
        analyze_kernel,
        "hh",
        [small, ("v", (WIDE, MARGIN), f32), ("v", square, bf16)],
        [pltpu.VMEM(square, f32), dma((2,))],
    )(*pinned(mask, rows_table))
    from_odd = lax.ppermute(to_odd, over, odd)
    to_even, own = call(own_kernel, "vvv", [small, small])(rest, to_odd, rows)
    from_even = lax.ppermute(to_even, over, even)
    mixed, goal, tables = call(
        prepare_kernel,
        "v" + "h" * 6,
        [("v", (PAIRS, 2, BAND, WIDE), f32), ("v", square, f32), ("v", tables.shape, bf16)],
        [
            pltpu.VMEM(square, f32),
            pltpu.VMEM((TABLE, KERN, 2, BAND, BAND), f32),
            smem((CONDS,), jnp.int32),
            smem((KERN, TABLE), f32),
            smem((TABLE,), f32),
            dma((4 + TSPLIT + CSPLIT,)),
        ],
    )(
        own,
        *pinned(condition_index, kernel_weight.T, dose_table, kernel_table, target, tables),
    )
    joined = call(join_kernel, "vv", [small])(own, from_odd)
    resist, grad, to_odd = call(
        window_kernel,
        "v" * 6,
        [("v", (CONDS, CORE, CORE), f32), small, ("v", (BAND + 8, WIDE), f32)],
    )(joined, from_even, goal, mixed, rows, tables)
    from_odd = lax.ppermute(to_odd, over, odd)
    from_even = lax.ppermute(grad, over, even)
    resist = call(store_kernel, "v", [("h", (CONDS, CORE, CORE), f32)], [dma((1,))])(resist)
    half = call(beside_kernel, "vvvv", [("v", (CORE, MARGIN), f32)])(grad, from_even, rows, tables)
    gradient = call(
        across_kernel,
        "vvvvv",
        [("h", square, f32)],
        [pltpu.VMEM((CORE, MARGIN), f32), dma((2,))],
    )(grad, from_odd, rows, tables, half)
    return (resist, gradient)


def solution(mesh):
    return jax.shard_map(
        local,
        mesh=mesh,
        in_specs=(P("win", "tile"), P("win", "tile"), P(), P(), P(), P()),
        out_specs=(P(None, "win", "tile"), P("win", "tile")),
        check_vma=False,
    )
```

```python
import math

import jax
import jax.numpy as jnp
import ml_dtypes
import numpy as np
from jax import lax
from jax.experimental import pallas as pl
from jax.experimental.pallas import tpu as pltpu
from jax.sharding import PartitionSpec as P

NPAD = 512
MARGIN = 128
BAND = 64
KERN = 2
TABLE = 4
CONDS = 2
CORE = 256
PAIRS = CONDS * KERN
WIDE = 2 * BAND
COARSE = 2 * BAND
STEP = NPAD // COARSE

steepness = 6.0
threshold = 0.3


def parts(table):
    high = table.astype(ml_dtypes.bfloat16)
    low = (table - high.astype(np.float64)).astype(ml_dtypes.bfloat16)
    return high, low


def waves(positions):
    frequency = np.arange(BAND)[:, None] - BAND // 2
    phase = (frequency * positions[None, :] % NPAD) * (2.0 * math.pi / NPAD)
    return np.concatenate([np.cos(phase), -np.sin(phase)], 0)


def interpolation():
    apart = np.arange(MARGIN, MARGIN + CORE)[:, None] - STEP * np.arange(COARSE)[None, :]
    frequency = np.arange(1, COARSE // 2)[:, None, None]
    total = 1.0 + 2.0 * np.cos((frequency * apart % NPAD) * (2.0 * math.pi / NPAD)).sum(0)
    total = total + np.cos((COARSE // 2 * apart % NPAD) * (2.0 * math.pi / NPAD))
    return total / COARSE


def side_by_side(table):
    return np.concatenate(parts(table), 1)


def later_tables(rows_table):
    points = waves(STEP * np.arange(COARSE))
    core = waves(np.arange(MARGIN, MARGIN + CORE))
    turned = np.concatenate([-core[BAND:], core[:BAND]], 0)
    finer = side_by_side(interpolation())
    return np.concatenate(
        [
            side_by_side(points), side_by_side(points.T), *parts(turned),
            finer, finer.T, rows_table.T, side_by_side(turned.T),
        ]
    )


def table_parts(tables):
    ends = np.cumsum([WIDE, COARSE, WIDE, WIDE, CORE, CORE, 2 * CORE])
    return [tables.at[int(end - size) : int(end)] for end, size in zip(ends, np.diff(ends, prepend=0))]


def halves(x):
    high = x.astype(jnp.bfloat16)
    return high, (x - high.astype(jnp.float32)).astype(jnp.bfloat16)


def dot(a, b):
    return jnp.dot(a, b, preferred_element_type=jnp.float32)


def turn(x):
    lane = lax.broadcasted_iota(jnp.int32, x.shape, 1)
    rolled = pltpu.roll(x, BAND, 1)
    return jnp.where(lane < BAND, -rolled, rolled)


def signs(shape):
    lane = lax.broadcasted_iota(jnp.int32, shape, 1)
    return jnp.where(lane % 2 == 0, 1.0, -1.0).astype(jnp.float32)


def stacked(x):
    return jnp.concatenate([x, -turn(x)], 0)


def strips(source, target, rows):
    return [
        (source.at[start : start + rows], target.at[start : start + rows])
        for start in range(0, source.shape[0], rows)
    ]


def copies(pairs, sems):
    moves = [pltpu.make_async_copy(a, b, sems.at[i]) for i, (a, b) in enumerate(pairs)]
    for move in moves:
        move.start()
    return moves


def place():
    tile, tiles = lax.axis_index("tile"), lax.axis_size("tile")
    return tile % 2 == 1, jnp.logical_or(tile == 0, tile == tiles - 1)


def across_lanes(a, b):
    return lax.dot_general(a, b, (((1,), (1,)), ((), ())), preferred_element_type=jnp.float32)


def half_spectrum(mask, rows, side):
    high, low = halves(mask)
    both = dot(rows[:WIDE], jnp.concatenate([high, low], 1))
    z = both[:, :MARGIN] + both[:, MARGIN:] + dot(rows[WIDE:], high)
    columns = rows[:, pl.ds(pl.multiple_of(side * MARGIN, MARGIN), MARGIN)]
    both = across_lanes(
        jnp.concatenate(halves(z), 1), jnp.concatenate([columns, columns], 1)
    )
    w = both[:, :WIDE] + both[:, WIDE:]
    return (w[:BAND] + turn(w[BAND:])) * signs((BAND, WIDE))


def analyze_kernel(
    mask_hbm, rows_hbm, table_hbm, target_hbm, odd_out, rest, rows, table, target, mask, sems
):
    odd, _ = place()
    side = jnp.where(odd, 1, 0)

    def half(side):
        return mask_hbm.at[:, pl.ds(pl.multiple_of(side * MARGIN, MARGIN), MARGIN)]

    moves = copies(
        [
            (half(side), mask),
            (rows_hbm, rows),
            (half(1 - side), rest),
            (target_hbm, target),
            *strips(table_hbm, table, TABLE // 2),
        ],
        sems,
    )
    for move in moves[:2]:
        move.wait()
    odd_out[...] = half_spectrum(mask[...], rows, side)
    for move in moves[2:]:
        move.wait()


def own_kernel(rest, odd_out, rows, even_out, own):
    odd, _ = place()
    even = half_spectrum(rest[...], rows, jnp.where(odd, 0, 1))
    even_out[...] = even
    own[...] = (even + odd_out[...]) * signs((BAND, WIDE))


def prepare_kernel(
    after, table, target, index_hbm, weight_hbm, dose_hbm, mixed, goal, index, weight, dose, sems
):
    moves = copies([(index_hbm, index), (weight_hbm, weight), (dose_hbm, dose)], sems)
    goal[...] = 1.0 - 2.0 * target[...]
    for move in moves:
        move.wait()
    for condition in range(CONDS):
        entry = index[condition]
        for k in range(KERN):
            scale = jnp.sqrt(
                jnp.full((1, WIDE), 0.5 * steepness * dose[entry] * weight[k, entry])
            ) * (1.0 / (NPAD * NPAD))
            for part in range(2):
                kernel = table[entry, k, part]
                doubled = jnp.concatenate([kernel, kernel], 1)
                mixed[condition * KERN + k, part] = doubled * scale


def join_kernel(own, odd_in, joined):
    _, alone = place()
    joined[...] = own[...] + jnp.where(alone, 0.0, odd_in[...])


def window_kernel(joined, even_in, goal, mixed, rows, tables, resist, grad, odd_out):
    points, points_t, turned_high, turned_low, finer, finer_t, back_both = table_parts(tables)
    spec = joined[...] + even_in[...]
    turned = turn(spec)
    out_high = jnp.concatenate([rows[:WIDE], turned_high[...]], 1)
    out_low = jnp.concatenate([rows[WIDE:], turned_low[...]], 1)
    out_twice = jnp.concatenate([out_high, out_high], 0)
    conditions = range(CONDS)

    def coarse_rows(condition):
        group = range(condition * KERN, (condition + 1) * KERN)
        top = jnp.concatenate([mixed[i, 0] * spec + mixed[i, 1] * turned for i in group], 1)
        bottom = jnp.concatenate([mixed[i, 1] * spec - mixed[i, 0] * turned for i in group], 1)
        high, low = halves(jnp.concatenate([top, bottom], 0))
        return dot(points_t[...], jnp.concatenate([high, high], 0)) + dot(points_t[:, :WIDE], low)

    def coarse_field(y):
        y = jnp.concatenate([y[:, k * WIDE : (k + 1) * WIDE] for k in range(KERN)], 0)
        high, low = halves(y)
        return dot(jnp.concatenate([high, low], 1), out_twice) + dot(high, out_low)

    def finer_rows(f):
        squares = f * f
        power = sum(
            squares[k * COARSE : (k + 1) * COARSE, c]
            for k in range(KERN)
            for c in (slice(0, CORE), slice(CORE, 2 * CORE))
        )
        high, low = halves(power - 0.5 * steepness * threshold)
        both = jnp.concatenate([high, low], 1)
        both = dot(finer[...], jnp.concatenate([both, both], 0))
        return both[:, :CORE] + both[:, CORE:]

    def print_and_drive(condition, power):
        t = jnp.tanh(power)
        resist[condition] = 0.5 + 0.5 * t
        return (t + goal[...]) * (1.0 - t * t)

    def coarser_rows(drive):
        high, low = halves(drive)
        both = dot(finer_t[:COARSE], jnp.concatenate([high, low], 1))
        return both[:, :CORE] + both[:, CORE:] + dot(finer_t[COARSE:], high)

    def back_columns(drive, f):
        drive = jnp.concatenate([drive, drive], 1)
        high, low = halves(jnp.concatenate([drive] * KERN, 0) * f)
        both = dot(high, back_both[...])
        q = both[:, :WIDE] + both[:, WIDE:] + dot(low, back_both[:, :WIDE])
        return jnp.concatenate([q[k * COARSE : (k + 1) * COARSE] for k in range(KERN)], 1)

    def back_rows(q):
        high, low = halves(q)
        return dot(points[...], jnp.concatenate([high, high], 0)) + dot(points[:, :COARSE], low)

    y = [coarse_rows(c) for c in conditions]
    fields = [coarse_field(x) for x in y]
    power = [finer_rows(f) for f in fields]
    drive = [print_and_drive(c, power[c]) for c in conditions]
    drive = [coarser_rows(x) for x in drive]
    q = [back_columns(drive[c], fields[c]) for c in conditions]
    u = [back_rows(x) for x in q]
    straight = jnp.zeros((BAND, WIDE), jnp.float32)
    crossed = jnp.zeros((BAND, WIDE), jnp.float32)
    for i in range(PAIRS):
        c = slice(i % KERN * WIDE, (i % KERN + 1) * WIDE)
        top, bottom = u[i // KERN][:BAND, c], u[i // KERN][BAND:, c]
        straight = straight + (mixed[i, 0] * top + mixed[i, 1] * bottom)
        crossed = crossed + (mixed[i, 0] * bottom - mixed[i, 1] * top)
    total = 2.0 * (straight + turn(crossed))
    grad[...] = total
    odd_out[:BAND] = total
    odd_out[BAND:] = total[: odd_out.shape[0] - BAND]


def synthesize(spec, rows, rows_t, side, out):
    both = jnp.concatenate(halves(stacked(spec)), 1)
    y = dot(rows_t[...], jnp.concatenate([both, both], 0))
    y = jnp.concatenate(halves(y[:, :WIDE] + y[:, WIDE:]), 1)
    c = pl.ds(pl.multiple_of(side * MARGIN, MARGIN), MARGIN)
    columns = jnp.concatenate([rows[:WIDE, c], rows[WIDE:, c]], 1)
    both = dot(y, jnp.concatenate([columns, columns], 0))
    out[...] = both[:, :MARGIN] + both[:, MARGIN:]


def store_kernel(resist, resist_hbm, sems):
    for move in copies([(resist, resist_hbm)], sems):
        move.wait()


def beside_kernel(own, even_in, rows, tables, half):
    odd, _ = place()
    spec = own[...] + even_in[...] * signs((BAND, WIDE))
    synthesize(spec, rows, table_parts(tables)[-1].at[:CORE], jnp.where(odd, 0, 1), half)


def across_kernel(own, odd_in, rows, tables, half, gradient_hbm, out, sems):
    odd, alone = place()
    side = jnp.where(odd, 1, 0)

    def columns(side):
        return gradient_hbm.at[:, pl.ds(pl.multiple_of(side * MARGIN, MARGIN), MARGIN)]

    moves = copies([(half, columns(1 - side))], sems)
    extra = jnp.where(alone, 0.0, odd_in[:BAND] * signs((BAND, WIDE)))
    synthesize(own[...] + extra, rows, table_parts(tables)[-1].at[:CORE], side, out)
    moves += copies([(out, columns(side))], sems.at[1:])
    for move in moves:
        move.wait()


def pinned(*arrays):
    return [pltpu.with_memory_space_constraint(jnp.asarray(a), pltpu.HBM) for a in arrays]


SPACES = {"v": pltpu.VMEM, "h": pltpu.HBM, "s": pltpu.SMEM}


def call(kernel, ins, outs, scratch=(), aliases=None, flops=10**6):
    shapes = [jax.ShapeDtypeStruct(shape, dtype) for _, shape, dtype in outs]
    specs = [pl.BlockSpec(memory_space=SPACES[o[0]]) for o in outs]
    return pl.pallas_call(
        kernel,
        out_shape=shapes if len(shapes) > 1 else shapes[0],
        in_specs=[pl.BlockSpec(memory_space=SPACES[i]) for i in ins],
        out_specs=specs if len(specs) > 1 else specs[0],
        scratch_shapes=list(scratch),
        input_output_aliases=aliases or {},
        compiler_params=pltpu.CompilerParams(vmem_limit_bytes=16 << 20),
        cost_estimate=pl.CostEstimate(flops=flops, bytes_accessed=1 << 16, transcendentals=0),
    )


def partners(windows, tiles):
    even = [(w * tiles + i, w * tiles + (i ^ 1)) for w in range(windows) for i in range(tiles)]
    odd = []
    for w in range(windows):
        base = w * tiles
        for i in range(1, tiles - 1, 2):
            odd += [(base + i, base + i + 1), (base + i + 1, base + i)]
        other = w ^ 1 if (w ^ 1) < windows else w
        for i in (0, tiles - 1):
            odd.append((base + i, other * tiles + i))
    return even, odd


def local(mask, target, kernel_table, kernel_weight, dose_table, condition_index):
    rows_table = np.concatenate(parts(waves(np.arange(MARGIN, MARGIN + CORE))), 0)
    tables = later_tables(rows_table)
    even, odd = partners(lax.axis_size("win"), lax.axis_size("tile"))
    over = ("win", "tile")
    f32, bf16 = jnp.float32, jnp.bfloat16
    small = ("v", (BAND, WIDE), f32)
    square = (CORE, CORE)
    dma, smem = pltpu.SemaphoreType.DMA, pltpu.SMEM
    half = ("v", (CORE, MARGIN), f32)
    to_odd, rest, rows, table, target = call(
        analyze_kernel,
        "hhhh",
        [small, half, ("v", square, bf16)] + [("v", x.shape, f32) for x in (kernel_table, target)],
        [pltpu.VMEM((CORE, MARGIN), f32), dma((6,))],
    )(*pinned(mask, rows_table, kernel_table, target))
    from_odd = lax.ppermute(to_odd, over, odd)
    to_even, own = call(own_kernel, "vvv", [small, small])(rest, to_odd, rows)
    from_even = lax.ppermute(to_even, over, even)
    mixed, goal = call(
        prepare_kernel,
        "vvvhhh",
        [("v", (PAIRS, 2, BAND, WIDE), f32), ("v", square, f32)],
        [
            smem((CONDS,), jnp.int32),
            smem((KERN, TABLE), f32),
            smem((TABLE,), f32),
            dma((3,)),
        ],
    )(own, table, target, *pinned(condition_index, kernel_weight.T, dose_table))
    joined = call(join_kernel, "vv", [small])(own, from_odd)
    resist, grad, to_odd = call(
        window_kernel,
        "v" * 6,
        [("v", (CONDS, CORE, CORE), f32), small, ("v", (BAND + 8, WIDE), f32)],
    )(joined, from_even, goal, mixed, rows, tables)
    from_odd = lax.ppermute(to_odd, over, odd)
    from_even = lax.ppermute(grad, over, even)
    resist = call(store_kernel, "v", [("h", (CONDS, CORE, CORE), f32)], [dma((1,))])(resist)
    made = call(beside_kernel, "vvvv", [half])(grad, from_even, rows, tables)
    gradient = call(
        across_kernel,
        "vvvvv",
        [("h", square, f32)],
        [pltpu.VMEM((CORE, MARGIN), f32), dma((2,))],
    )(grad, from_odd, rows, tables, made)
    return (resist, gradient)


def solution(mesh):
    return jax.shard_map(
        local,
        mesh=mesh,
        in_specs=(P("win", "tile"), P("win", "tile"), P(), P(), P(), P()),
        out_specs=(P(None, "win", "tile"), P("win", "tile")),
        check_vma=False,
    )
```

```python
import math

import jax
import jax.numpy as jnp
import ml_dtypes
import numpy as np
from jax import lax
from jax.experimental import pallas as pl
from jax.experimental.pallas import tpu as pltpu
from jax.sharding import PartitionSpec as P

NPAD = 512
MARGIN = 128
BAND = 64
KERN = 2
TABLE = 4
CONDS = 2
CORE = 256
PAIRS = CONDS * KERN
WIDE = 2 * BAND
COARSE = 2 * BAND
STEP = NPAD // COARSE

steepness = 6.0
threshold = 0.3


def parts(table):
    high = table.astype(ml_dtypes.bfloat16)
    low = (table - high.astype(np.float64)).astype(ml_dtypes.bfloat16)
    return high, low


def waves(positions):
    frequency = np.arange(BAND)[:, None] - BAND // 2
    phase = (frequency * positions[None, :] % NPAD) * (2.0 * math.pi / NPAD)
    return np.concatenate([np.cos(phase), -np.sin(phase)], 0)


def interpolation():
    apart = np.arange(MARGIN, MARGIN + CORE)[:, None] - STEP * np.arange(COARSE)[None, :]
    frequency = np.arange(1, COARSE // 2)[:, None, None]
    total = 1.0 + 2.0 * np.cos((frequency * apart % NPAD) * (2.0 * math.pi / NPAD)).sum(0)
    total = total + np.cos((COARSE // 2 * apart % NPAD) * (2.0 * math.pi / NPAD))
    return total / COARSE


def side_by_side(table):
    return np.concatenate(parts(table), 1)


def later_tables(rows_table):
    points = waves(STEP * np.arange(COARSE))
    core = waves(np.arange(MARGIN, MARGIN + CORE))
    turned = np.concatenate([-core[BAND:], core[:BAND]], 0)
    finer = side_by_side(interpolation())
    return np.concatenate(
        [
            side_by_side(points), side_by_side(points.T), *parts(turned),
            finer, finer.T, rows_table.T, side_by_side(turned.T),
        ]
    )


def table_parts(tables):
    ends = np.cumsum([WIDE, COARSE, WIDE, WIDE, CORE, CORE, 2 * CORE])
    return [tables.at[int(end - size) : int(end)] for end, size in zip(ends, np.diff(ends, prepend=0))]


def halves(x):
    high = x.astype(jnp.bfloat16)
    return high, (x - high.astype(jnp.float32)).astype(jnp.bfloat16)


def dot(a, b):
    return jnp.dot(a, b, preferred_element_type=jnp.float32)


def turn(x):
    lane = lax.broadcasted_iota(jnp.int32, x.shape, 1)
    rolled = pltpu.roll(x, BAND, 1)
    return jnp.where(lane < BAND, -rolled, rolled)


def signs(shape):
    lane = lax.broadcasted_iota(jnp.int32, shape, 1)
    return jnp.where(lane % 2 == 0, 1.0, -1.0).astype(jnp.float32)


def stacked(x):
    return jnp.concatenate([x, -turn(x)], 0)


def strips(source, target, rows):
    return [
        (source.at[start : start + rows], target.at[start : start + rows])
        for start in range(0, source.shape[0], rows)
    ]


def copies(pairs, sems):
    moves = [pltpu.make_async_copy(a, b, sems.at[i]) for i, (a, b) in enumerate(pairs)]
    for move in moves:
        move.start()
    return moves


def place():
    tile, tiles = lax.axis_index("tile"), lax.axis_size("tile")
    return tile % 2 == 1, jnp.logical_or(tile == 0, tile == tiles - 1)


def across_lanes(a, b):
    return lax.dot_general(a, b, (((1,), (1,)), ((), ())), preferred_element_type=jnp.float32)


def half_spectrum(mask, rows, side):
    high, low = halves(mask)
    both = dot(rows[:WIDE], jnp.concatenate([high, low], 1))
    z = both[:, :MARGIN] + both[:, MARGIN:] + dot(rows[WIDE:], high)
    columns = rows[:, pl.ds(pl.multiple_of(side * MARGIN, MARGIN), MARGIN)]
    both = across_lanes(
        jnp.concatenate(halves(z), 1), jnp.concatenate([columns, columns], 1)
    )
    w = both[:, :WIDE] + both[:, WIDE:]
    return (w[:BAND] + turn(w[BAND:])) * signs((BAND, WIDE))


def analyze_kernel(
    mask_hbm, rows_hbm, table_hbm, target_hbm, odd_out, rest, rows, table, target, mask, sems
):
    odd, _ = place()
    side = jnp.where(odd, 1, 0)

    def half(side):
        return mask_hbm.at[:, pl.ds(pl.multiple_of(side * MARGIN, MARGIN), MARGIN)]

    moves = copies(
        [
            (half(side), mask),
            (rows_hbm, rows),
            (half(1 - side), rest),
            (target_hbm, target),
            *strips(table_hbm, table, TABLE // 2),
        ],
        sems,
    )
    for move in moves[:2]:
        move.wait()
    odd_out[...] = half_spectrum(mask[...], rows, side)
    for move in moves[2:]:
        move.wait()


def own_kernel(rest, odd_out, rows, even_out, own):
    odd, _ = place()
    even = half_spectrum(rest[...], rows, jnp.where(odd, 0, 1))
    even_out[...] = even
    own[...] = (even + odd_out[...]) * signs((BAND, WIDE))


def prepare_kernel(
    after, table, target, index_hbm, weight_hbm, dose_hbm, mixed, goal, index, weight, dose, sems
):
    moves = copies([(index_hbm, index), (weight_hbm, weight), (dose_hbm, dose)], sems)
    goal[...] = 1.0 - 2.0 * target[...]
    for move in moves:
        move.wait()
    for condition in range(CONDS):
        entry = index[condition]
        for k in range(KERN):
            scale = jnp.sqrt(
                jnp.full((1, WIDE), 0.5 * steepness * dose[entry] * weight[k, entry])
            ) * (1.0 / (NPAD * NPAD))
            for part in range(2):
                kernel = table[entry, k, part]
                doubled = jnp.concatenate([kernel, kernel], 1)
                mixed[condition * KERN + k, part] = doubled * scale


def join_kernel(own, odd_in, joined):
    _, alone = place()
    joined[...] = own[...] + jnp.where(alone, 0.0, odd_in[...])


def window_kernel(joined, even_in, goal, mixed, rows, tables, resist, grad, odd_out):
    points, points_t, turned_high, turned_low, finer, finer_t, back_both = table_parts(tables)
    spec = joined[...] + even_in[...]
    turned = turn(spec)
    out_high = jnp.concatenate([rows[:WIDE], turned_high[...]], 1)
    out_low = jnp.concatenate([rows[WIDE:], turned_low[...]], 1)
    out_twice = jnp.concatenate([out_high, out_high], 0)
    conditions = range(CONDS)

    def coarse_rows(condition):
        group = range(condition * KERN, (condition + 1) * KERN)
        top = jnp.concatenate([mixed[i, 0] * spec + mixed[i, 1] * turned for i in group], 1)
        bottom = jnp.concatenate([mixed[i, 1] * spec - mixed[i, 0] * turned for i in group], 1)
        high, low = halves(jnp.concatenate([top, bottom], 0))
        return dot(points_t[...], jnp.concatenate([high, high], 0)) + dot(points_t[:, :WIDE], low)

    def coarse_field(y):
        y = jnp.concatenate([y[:, k * WIDE : (k + 1) * WIDE] for k in range(PAIRS)], 0)
        high, low = halves(y)
        return dot(jnp.concatenate([high, low], 1), out_twice) + dot(high, out_low)

    def finer_rows(f):
        squares = f * f
        power = sum(
            squares[k * COARSE : (k + 1) * COARSE, c]
            for k in range(KERN)
            for c in (slice(0, CORE), slice(CORE, 2 * CORE))
        )
        high, low = halves(power - 0.5 * steepness * threshold)
        both = jnp.concatenate([high, low], 1)
        both = dot(finer[...], jnp.concatenate([both, both], 0))
        return both[:, :CORE] + both[:, CORE:]

    def print_and_drive(condition, power):
        t = jnp.tanh(power)
        resist[condition] = 0.5 + 0.5 * t
        return (t + goal[...]) * (1.0 - t * t)

    def coarser_rows(drive):
        high, low = halves(drive)
        both = dot(finer_t[:COARSE], jnp.concatenate([high, low], 1))
        return both[:, :CORE] + both[:, CORE:] + dot(finer_t[COARSE:], high)

    def back_columns(drive, f):
        drive = jnp.concatenate([drive, drive], 1)
        high, low = halves(jnp.concatenate([drive] * KERN, 0) * f)
        both = dot(high, back_both[...])
        q = both[:, :WIDE] + both[:, WIDE:] + dot(low, back_both[:, :WIDE])
        return jnp.concatenate([q[k * COARSE : (k + 1) * COARSE] for k in range(KERN)], 1)

    def back_rows(q):
        high, low = halves(q)
        return dot(points[...], jnp.concatenate([high, high], 0)) + dot(points[:, :COARSE], low)

    y = [coarse_rows(c) for c in conditions]
    fields = coarse_field(jnp.concatenate(y, 1))
    fields = [fields[c * KERN * COARSE : (c + 1) * KERN * COARSE] for c in conditions]
    power = [finer_rows(f) for f in fields]
    drive = [print_and_drive(c, power[c]) for c in conditions]
    drive = [coarser_rows(x) for x in drive]
    q = [back_columns(drive[c], fields[c]) for c in conditions]
    u = [back_rows(x) for x in q]
    straight = jnp.zeros((BAND, WIDE), jnp.float32)
    crossed = jnp.zeros((BAND, WIDE), jnp.float32)
    for i in range(PAIRS):
        c = slice(i % KERN * WIDE, (i % KERN + 1) * WIDE)
        top, bottom = u[i // KERN][:BAND, c], u[i // KERN][BAND:, c]
        straight = straight + (mixed[i, 0] * top + mixed[i, 1] * bottom)
        crossed = crossed + (mixed[i, 0] * bottom - mixed[i, 1] * top)
    total = 2.0 * (straight + turn(crossed))
    grad[...] = total
    odd_out[...] = total


def synthesize(spec, rows, rows_t, side, out):
    both = jnp.concatenate(halves(stacked(spec)), 1)
    y = dot(rows_t[...], jnp.concatenate([both, both], 0))
    y = jnp.concatenate(halves(y[:, :WIDE] + y[:, WIDE:]), 1)
    c = pl.ds(pl.multiple_of(side * MARGIN, MARGIN), MARGIN)
    columns = jnp.concatenate([rows[:WIDE, c], rows[WIDE:, c]], 1)
    both = dot(y, jnp.concatenate([columns, columns], 0))
    out[...] = both[:, :MARGIN] + both[:, MARGIN:]


def store_kernel(resist, resist_hbm, sems):
    for move in copies([(resist, resist_hbm)], sems):
        move.wait()


def beside_kernel(own, even_in, rows, tables, half):
    odd, _ = place()
    spec = own[...] + even_in[...] * signs((BAND, WIDE))
    synthesize(spec, rows, table_parts(tables)[-1].at[:CORE], jnp.where(odd, 0, 1), half)


def across_kernel(own, odd_in, rows, tables, half, gradient_hbm, out, sems):
    odd, alone = place()
    side = jnp.where(odd, 1, 0)

    def columns(side):
        return gradient_hbm.at[:, pl.ds(pl.multiple_of(side * MARGIN, MARGIN), MARGIN)]

    moves = copies([(half, columns(1 - side))], sems)
    extra = jnp.where(alone, 0.0, odd_in[...] * signs((BAND, WIDE)))
    rows_t = table_parts(tables)[-1]
    for i in range(2):
        r = slice(i * CORE // 2, (i + 1) * CORE // 2)
        synthesize(own[...] + extra, rows, rows_t.at[r], side, out.at[r])
        moves += copies([(out.at[r], columns(side).at[r])], sems.at[1 + i :])
    for move in moves:
        move.wait()


def pinned(*arrays):
    return [pltpu.with_memory_space_constraint(jnp.asarray(a), pltpu.HBM) for a in arrays]


SPACES = {"v": pltpu.VMEM, "h": pltpu.HBM, "s": pltpu.SMEM}


def call(kernel, ins, outs, scratch=(), aliases=None, flops=10**6):
    shapes = [jax.ShapeDtypeStruct(shape, dtype) for _, shape, dtype in outs]
    specs = [pl.BlockSpec(memory_space=SPACES[o[0]]) for o in outs]
    return pl.pallas_call(
        kernel,
        out_shape=shapes if len(shapes) > 1 else shapes[0],
        in_specs=[pl.BlockSpec(memory_space=SPACES[i]) for i in ins],
        out_specs=specs if len(specs) > 1 else specs[0],
        scratch_shapes=list(scratch),
        input_output_aliases=aliases or {},
        compiler_params=pltpu.CompilerParams(vmem_limit_bytes=16 << 20),
        cost_estimate=pl.CostEstimate(flops=flops, bytes_accessed=1 << 16, transcendentals=0),
    )


def partners(windows, tiles):
    even = [(w * tiles + i, w * tiles + (i ^ 1)) for w in range(windows) for i in range(tiles)]
    odd = []
    for w in range(windows):
        base = w * tiles
        for i in range(1, tiles - 1, 2):
            odd += [(base + i, base + i + 1), (base + i + 1, base + i)]
        other = w ^ 1 if (w ^ 1) < windows else w
        for i in (0, tiles - 1):
            odd.append((base + i, other * tiles + i))
    return even, odd


def local(mask, target, kernel_table, kernel_weight, dose_table, condition_index):
    rows_table = np.concatenate(parts(waves(np.arange(MARGIN, MARGIN + CORE))), 0)
    tables = later_tables(rows_table)
    even, odd = partners(lax.axis_size("win"), lax.axis_size("tile"))
    over = ("win", "tile")
    f32, bf16 = jnp.float32, jnp.bfloat16
    small = ("v", (BAND, WIDE), f32)
    square = (CORE, CORE)
    dma, smem = pltpu.SemaphoreType.DMA, pltpu.SMEM
    half = ("v", (CORE, MARGIN), f32)
    to_odd, rest, rows, table, target = call(
        analyze_kernel,
        "hhhh",
        [small, half, ("v", square, bf16)] + [("v", x.shape, f32) for x in (kernel_table, target)],
        [pltpu.VMEM((CORE, MARGIN), f32), dma((6,))],
    )(*pinned(mask, rows_table, kernel_table, target))
    from_odd = lax.ppermute(to_odd, over, odd)
    to_even, own = call(own_kernel, "vvv", [small, small])(rest, to_odd, rows)
    from_even = lax.ppermute(to_even, over, even)
    mixed, goal = call(
        prepare_kernel,
        "vvvhhh",
        [("v", (PAIRS, 2, BAND, WIDE), f32), ("v", square, f32)],
        [
            smem((CONDS,), jnp.int32),
            smem((KERN, TABLE), f32),
            smem((TABLE,), f32),
            dma((3,)),
        ],
    )(own, table, target, *pinned(condition_index, kernel_weight.T, dose_table))
    joined = call(join_kernel, "vv", [small])(own, from_odd)
    resist, grad, to_odd = call(
        window_kernel,
        "v" * 6,
        [("v", (CONDS, CORE, CORE), f32), small, small],
    )(joined, from_even, goal, mixed, rows, tables)
    from_odd = lax.ppermute(to_odd, over, odd)
    from_even = lax.ppermute(grad, over, even)
    resist = call(store_kernel, "v", [("h", (CONDS, CORE, CORE), f32)], [dma((1,))])(resist)
    made = call(beside_kernel, "vvvv", [half])(grad, from_even, rows, tables)
    gradient = call(
        across_kernel,
        "vvvvv",
        [("h", square, f32)],
        [pltpu.VMEM((CORE, MARGIN), f32), dma((3,))],
    )(grad, from_odd, rows, tables, made)
    return (resist, gradient)


def solution(mesh):
    return jax.shard_map(
        local,
        mesh=mesh,
        in_specs=(P("win", "tile"), P("win", "tile"), P(), P(), P(), P()),
        out_specs=(P(None, "win", "tile"), P("win", "tile")),
        check_vma=False,
    )
```

```python
import math

import jax
import jax.numpy as jnp
import ml_dtypes
import numpy as np
from jax import lax
from jax.experimental import pallas as pl
from jax.experimental.pallas import tpu as pltpu
from jax.sharding import PartitionSpec as P

NPAD = 512
MARGIN = 128
BAND = 64
KERN = 2
TABLE = 4
CONDS = 2
CORE = 256
PAIRS = CONDS * KERN
WIDE = 2 * BAND
COARSE = 2 * BAND
STEP = NPAD // COARSE

steepness = 6.0
threshold = 0.3


def parts(table):
    high = table.astype(ml_dtypes.bfloat16)
    low = (table - high.astype(np.float64)).astype(ml_dtypes.bfloat16)
    return high, low


def waves(positions):
    frequency = np.arange(BAND)[:, None] - BAND // 2
    phase = (frequency * positions[None, :] % NPAD) * (2.0 * math.pi / NPAD)
    return np.concatenate([np.cos(phase), -np.sin(phase)], 0)


def interpolation():
    apart = np.arange(MARGIN, MARGIN + CORE)[:, None] - STEP * np.arange(COARSE)[None, :]
    frequency = np.arange(1, COARSE // 2)[:, None, None]
    total = 1.0 + 2.0 * np.cos((frequency * apart % NPAD) * (2.0 * math.pi / NPAD)).sum(0)
    total = total + np.cos((COARSE // 2 * apart % NPAD) * (2.0 * math.pi / NPAD))
    return total / COARSE


def side_by_side(table):
    return np.concatenate(parts(table), 1)


def later_tables(rows_table):
    points = waves(STEP * np.arange(COARSE))
    core = waves(np.arange(MARGIN, MARGIN + CORE))
    turned = np.concatenate([-core[BAND:], core[:BAND]], 0)
    finer = side_by_side(interpolation())
    return np.concatenate(
        [
            side_by_side(points), side_by_side(points.T), *parts(turned),
            finer, finer.T, rows_table.T, side_by_side(turned.T),
        ]
    )


def table_parts(tables):
    ends = np.cumsum([WIDE, COARSE, WIDE, WIDE, CORE, CORE, 2 * CORE])
    return [tables.at[int(end - size) : int(end)] for end, size in zip(ends, np.diff(ends, prepend=0))]


def halves(x):
    high = x.astype(jnp.bfloat16)
    return high, (x - high.astype(jnp.float32)).astype(jnp.bfloat16)


def dot(a, b):
    return jnp.dot(a, b, preferred_element_type=jnp.float32)


def turn(x):
    lane = lax.broadcasted_iota(jnp.int32, x.shape, 1)
    rolled = pltpu.roll(x, BAND, 1)
    return jnp.where(lane < BAND, -rolled, rolled)


def signs(shape):
    lane = lax.broadcasted_iota(jnp.int32, shape, 1)
    return jnp.where(lane % 2 == 0, 1.0, -1.0).astype(jnp.float32)


def stacked(x):
    return jnp.concatenate([x, -turn(x)], 0)


def strips(source, target, rows):
    return [
        (source.at[start : start + rows], target.at[start : start + rows])
        for start in range(0, source.shape[0], rows)
    ]


def copies(pairs, sems):
    moves = [pltpu.make_async_copy(a, b, sems.at[i]) for i, (a, b) in enumerate(pairs)]
    for move in moves:
        move.start()
    return moves


def place():
    tile, tiles = lax.axis_index("tile"), lax.axis_size("tile")
    return tile % 2 == 1, jnp.logical_or(tile == 0, tile == tiles - 1)


def across_lanes(a, b):
    return lax.dot_general(a, b, (((1,), (1,)), ((), ())), preferred_element_type=jnp.float32)


def half_spectrum(window, rows, side):
    high, low = halves(window[:, pl.ds(pl.multiple_of(side * MARGIN, MARGIN), MARGIN)])
    both = dot(rows[:WIDE], jnp.concatenate([high, low], 1))
    z = both[:, :MARGIN] + both[:, MARGIN:] + dot(rows[WIDE:], high)
    columns = rows[:, pl.ds(pl.multiple_of(side * MARGIN, MARGIN), MARGIN)]
    both = across_lanes(
        jnp.concatenate(halves(z), 1), jnp.concatenate([columns, columns], 1)
    )
    w = both[:, :WIDE] + both[:, WIDE:]
    return (w[:BAND] + turn(w[BAND:])) * signs((BAND, WIDE))


def analyze_kernel(
    mask_hbm, rows_hbm, table_hbm, target_hbm, odd_out, mask, rows, table, target, sems
):
    odd, _ = place()
    moves = copies(
        [
            (mask_hbm, mask),
            (rows_hbm, rows),
            (target_hbm, target),
            *strips(table_hbm, table, TABLE // 2),
        ],
        sems,
    )
    for move in moves[:2]:
        move.wait()
    odd_out[...] = half_spectrum(mask, rows, jnp.where(odd, 1, 0))
    for move in moves[2:]:
        move.wait()


def own_kernel(mask, odd_out, rows, even_out, own):
    odd, _ = place()
    even = half_spectrum(mask, rows, jnp.where(odd, 0, 1))
    even_out[...] = even
    own[...] = (even + odd_out[...]) * signs((BAND, WIDE))


def prepare_kernel(
    after, table, target, index_hbm, weight_hbm, dose_hbm, mixed, goal, index, weight, dose, sems
):
    moves = copies([(index_hbm, index), (weight_hbm, weight), (dose_hbm, dose)], sems)
    goal[...] = 1.0 - 2.0 * target[...]
    for move in moves:
        move.wait()
    for condition in range(CONDS):
        entry = index[condition]
        for k in range(KERN):
            scale = jnp.sqrt(
                jnp.full((1, WIDE), 0.5 * steepness * dose[entry] * weight[k, entry])
            ) * (1.0 / (NPAD * NPAD))
            for part in range(2):
                kernel = table[entry, k, part]
                doubled = jnp.concatenate([kernel, kernel], 1)
                mixed[condition * KERN + k, part] = doubled * scale


def join_kernel(own, odd_in, joined):
    _, alone = place()
    joined[...] = own[...] + jnp.where(alone, 0.0, odd_in[...])


def window_kernel(joined, even_in, goal, mixed, rows, tables, resist, grad, odd_out):
    points, points_t, turned_high, turned_low, finer, finer_t, back_both = table_parts(tables)
    spec = joined[...] + even_in[...]
    turned = turn(spec)
    out_high = jnp.concatenate([rows[:WIDE], turned_high[...]], 1)
    out_low = jnp.concatenate([rows[WIDE:], turned_low[...]], 1)
    out_twice = jnp.concatenate([out_high, out_high], 0)
    conditions = range(CONDS)

    def coarse_rows(condition):
        group = range(condition * KERN, (condition + 1) * KERN)
        top = jnp.concatenate([mixed[i, 0] * spec + mixed[i, 1] * turned for i in group], 1)
        bottom = jnp.concatenate([mixed[i, 1] * spec - mixed[i, 0] * turned for i in group], 1)
        high, low = halves(jnp.concatenate([top, bottom], 0))
        return dot(points_t[...], jnp.concatenate([high, high], 0)) + dot(points_t[:, :WIDE], low)

    def coarse_field(y):
        y = jnp.concatenate([y[:, k * WIDE : (k + 1) * WIDE] for k in range(KERN)], 0)
        high, low = halves(y)
        return dot(jnp.concatenate([high, low], 1), out_twice) + dot(high, out_low)

    def finer_rows(f):
        squares = f * f
        power = sum(
            squares[k * COARSE : (k + 1) * COARSE, c]
            for k in range(KERN)
            for c in (slice(0, CORE), slice(CORE, 2 * CORE))
        )
        high, low = halves(power - 0.5 * steepness * threshold)
        both = jnp.concatenate([high, low], 1)
        both = dot(finer[...], jnp.concatenate([both, both], 0))
        return both[:, :CORE] + both[:, CORE:]

    def print_and_drive(condition, power):
        t = jnp.tanh(power)
        resist[condition] = 0.5 + 0.5 * t
        return (t + goal[...]) * (1.0 - t * t)

    def coarser_rows(drive):
        high, low = halves(drive)
        both = dot(finer_t[:COARSE], jnp.concatenate([high, low], 1))
        return both[:, :CORE] + both[:, CORE:] + dot(finer_t[COARSE:], high)

    def back_columns(drive, f):
        drive = jnp.concatenate([drive, drive], 1)
        high, low = halves(jnp.concatenate([drive] * KERN, 0) * f)
        both = dot(high, back_both[...])
        q = both[:, :WIDE] + both[:, WIDE:] + dot(low, back_both[:, :WIDE])
        return jnp.concatenate([q[k * COARSE : (k + 1) * COARSE] for k in range(KERN)], 1)

    def back_rows(q):
        high, low = halves(q)
        return dot(points[...], jnp.concatenate([high, high], 0)) + dot(points[:, :COARSE], low)

    y = [coarse_rows(c) for c in conditions]
    fields = [coarse_field(x) for x in y]
    power = [finer_rows(f) for f in fields]
    drive = [print_and_drive(c, power[c]) for c in conditions]
    drive = [coarser_rows(x) for x in drive]
    q = [back_columns(drive[c], fields[c]) for c in conditions]
    u = [back_rows(x) for x in q]
    straight = jnp.zeros((BAND, WIDE), jnp.float32)
    crossed = jnp.zeros((BAND, WIDE), jnp.float32)
    for i in range(PAIRS):
        c = slice(i % KERN * WIDE, (i % KERN + 1) * WIDE)
        top, bottom = u[i // KERN][:BAND, c], u[i // KERN][BAND:, c]
        straight = straight + (mixed[i, 0] * top + mixed[i, 1] * bottom)
        crossed = crossed + (mixed[i, 0] * bottom - mixed[i, 1] * top)
    total = 2.0 * (straight + turn(crossed))
    grad[...] = total
    odd_out[:BAND] = total
    odd_out[BAND:] = total[: odd_out.shape[0] - BAND]


def synthesize(spec, rows, rows_t, side, out):
    both = jnp.concatenate(halves(stacked(spec)), 1)
    y = dot(rows_t[...], jnp.concatenate([both, both], 0))
    y = jnp.concatenate(halves(y[:, :WIDE] + y[:, WIDE:]), 1)
    c = pl.ds(pl.multiple_of(side * MARGIN, MARGIN), MARGIN)
    columns = jnp.concatenate([rows[:WIDE, c], rows[WIDE:, c]], 1)
    both = dot(y, jnp.concatenate([columns, columns], 0))
    out[...] = both[:, :MARGIN] + both[:, MARGIN:]


def store_kernel(resist, resist_hbm, sems):
    for move in copies([(resist, resist_hbm)], sems):
        move.wait()


def beside_kernel(own, even_in, rows, tables, half):
    odd, _ = place()
    spec = own[...] + even_in[...] * signs((BAND, WIDE))
    synthesize(spec, rows, table_parts(tables)[-1].at[:CORE], jnp.where(odd, 0, 1), half)


def across_kernel(own, odd_in, rows, tables, half, gradient_hbm, out, sems):
    odd, alone = place()
    side = jnp.where(odd, 1, 0)

    def columns(side):
        return gradient_hbm.at[:, pl.ds(pl.multiple_of(side * MARGIN, MARGIN), MARGIN)]

    moves = copies([(half, columns(1 - side))], sems)
    extra = jnp.where(alone, 0.0, odd_in[:BAND] * signs((BAND, WIDE)))
    synthesize(own[...] + extra, rows, table_parts(tables)[-1].at[:CORE], side, out)
    moves += copies([(out, columns(side))], sems.at[1:])
    for move in moves:
        move.wait()


def pinned(*arrays):
    return [pltpu.with_memory_space_constraint(jnp.asarray(a), pltpu.HBM) for a in arrays]


SPACES = {"v": pltpu.VMEM, "h": pltpu.HBM, "s": pltpu.SMEM}


def call(kernel, ins, outs, scratch=(), aliases=None, flops=10**6):
    shapes = [jax.ShapeDtypeStruct(shape, dtype) for _, shape, dtype in outs]
    specs = [pl.BlockSpec(memory_space=SPACES[o[0]]) for o in outs]
    return pl.pallas_call(
        kernel,
        out_shape=shapes if len(shapes) > 1 else shapes[0],
        in_specs=[pl.BlockSpec(memory_space=SPACES[i]) for i in ins],
        out_specs=specs if len(specs) > 1 else specs[0],
        scratch_shapes=list(scratch),
        input_output_aliases=aliases or {},
        compiler_params=pltpu.CompilerParams(vmem_limit_bytes=16 << 20),
        cost_estimate=pl.CostEstimate(flops=flops, bytes_accessed=1 << 16, transcendentals=0),
    )


def partners(windows, tiles):
    even = [(w * tiles + i, w * tiles + (i ^ 1)) for w in range(windows) for i in range(tiles)]
    odd = []
    for w in range(windows):
        base = w * tiles
        for i in range(1, tiles - 1, 2):
            odd += [(base + i, base + i + 1), (base + i + 1, base + i)]
        other = w ^ 1 if (w ^ 1) < windows else w
        for i in (0, tiles - 1):
            odd.append((base + i, other * tiles + i))
    return even, odd


def local(mask, target, kernel_table, kernel_weight, dose_table, condition_index):
    rows_table = np.concatenate(parts(waves(np.arange(MARGIN, MARGIN + CORE))), 0)
    tables = later_tables(rows_table)
    even, odd = partners(lax.axis_size("win"), lax.axis_size("tile"))
    over = ("win", "tile")
    f32, bf16 = jnp.float32, jnp.bfloat16
    small = ("v", (BAND, WIDE), f32)
    square = (CORE, CORE)
    dma, smem = pltpu.SemaphoreType.DMA, pltpu.SMEM
    half = ("v", (CORE, MARGIN), f32)
    to_odd, window, rows, table, target = call(
        analyze_kernel,
        "hhhh",
        [small, ("v", square, f32), ("v", square, bf16)] + [("v", x.shape, f32) for x in (kernel_table, target)],
        [dma((5,))],
    )(*pinned(mask, rows_table, kernel_table, target))
    from_odd = lax.ppermute(to_odd, over, odd)
    to_even, own = call(own_kernel, "vvv", [small, small])(window, to_odd, rows)
    from_even = lax.ppermute(to_even, over, even)
    mixed, goal = call(
        prepare_kernel,
        "vvvhhh",
        [("v", (PAIRS, 2, BAND, WIDE), f32), ("v", square, f32)],
        [
            smem((CONDS,), jnp.int32),
            smem((KERN, TABLE), f32),
            smem((TABLE,), f32),
            dma((3,)),
        ],
    )(own, table, target, *pinned(condition_index, kernel_weight.T, dose_table))
    joined = call(join_kernel, "vv", [small])(own, from_odd)
    resist, grad, to_odd = call(
        window_kernel,
        "v" * 6,
        [("v", (CONDS, CORE, CORE), f32), small, ("v", (BAND + 8, WIDE), f32)],
    )(joined, from_even, goal, mixed, rows, tables)
    from_odd = lax.ppermute(to_odd, over, odd)
    from_even = lax.ppermute(grad, over, even)
    resist = call(store_kernel, "v", [("h", (CONDS, CORE, CORE), f32)], [dma((1,))])(resist)
    made = call(beside_kernel, "vvvv", [half])(grad, from_even, rows, tables)
    gradient = call(
        across_kernel,
        "vvvvv",
        [("h", square, f32)],
        [pltpu.VMEM((CORE, MARGIN), f32), dma((2,))],
    )(grad, from_odd, rows, tables, made)
    return (resist, gradient)


def solution(mesh):
    return jax.shard_map(
        local,
        mesh=mesh,
        in_specs=(P("win", "tile"), P("win", "tile"), P(), P(), P(), P()),
        out_specs=(P(None, "win", "tile"), P("win", "tile")),
        check_vma=False,
    )
```

```python
import math

import jax
import jax.numpy as jnp
import ml_dtypes
import numpy as np
from jax import lax
from jax.experimental import pallas as pl
from jax.experimental.pallas import tpu as pltpu
from jax.sharding import PartitionSpec as P

NPAD = 512
MARGIN = 128
BAND = 64
KERN = 2
TABLE = 4
CONDS = 2
CORE = 256
PAIRS = CONDS * KERN
WIDE = 2 * BAND
COARSE = 2 * BAND
STEP = NPAD // COARSE

steepness = 6.0
threshold = 0.3


def parts(table):
    high = table.astype(ml_dtypes.bfloat16)
    low = (table - high.astype(np.float64)).astype(ml_dtypes.bfloat16)
    return high, low


def waves(positions):
    frequency = np.arange(BAND)[:, None] - BAND // 2
    phase = (frequency * positions[None, :] % NPAD) * (2.0 * math.pi / NPAD)
    return np.concatenate([np.cos(phase), -np.sin(phase)], 0)


def interpolation():
    apart = np.arange(MARGIN, MARGIN + CORE)[:, None] - STEP * np.arange(COARSE)[None, :]
    frequency = np.arange(1, COARSE // 2)[:, None, None]
    total = 1.0 + 2.0 * np.cos((frequency * apart % NPAD) * (2.0 * math.pi / NPAD)).sum(0)
    total = total + np.cos((COARSE // 2 * apart % NPAD) * (2.0 * math.pi / NPAD))
    return total / COARSE


def side_by_side(table):
    return np.concatenate(parts(table), 1)


def later_tables(rows_table):
    points = waves(STEP * np.arange(COARSE))
    core = waves(np.arange(MARGIN, MARGIN + CORE))
    turned = np.concatenate([-core[BAND:], core[:BAND]], 0)
    finer = side_by_side(interpolation())
    return np.concatenate(
        [
            side_by_side(points), side_by_side(points.T), *parts(turned),
            finer, finer.T, rows_table.T, side_by_side(turned.T),
        ]
    )


def table_parts(tables):
    ends = np.cumsum([WIDE, COARSE, WIDE, WIDE, CORE, CORE, 2 * CORE])
    return [tables.at[int(end - size) : int(end)] for end, size in zip(ends, np.diff(ends, prepend=0))]


def halves(x):
    high = x.astype(jnp.bfloat16)
    return high, (x - high.astype(jnp.float32)).astype(jnp.bfloat16)


def dot(a, b):
    return jnp.dot(a, b, preferred_element_type=jnp.float32)


def turn(x):
    lane = lax.broadcasted_iota(jnp.int32, x.shape, 1)
    rolled = pltpu.roll(x, BAND, 1)
    return jnp.where(lane < BAND, -rolled, rolled)


def signs(shape):
    lane = lax.broadcasted_iota(jnp.int32, shape, 1)
    return jnp.where(lane % 2 == 0, 1.0, -1.0).astype(jnp.float32)


def stacked(x):
    return jnp.concatenate([x, -turn(x)], 0)


def strips(source, target, rows):
    return [
        (source.at[start : start + rows], target.at[start : start + rows])
        for start in range(0, source.shape[0], rows)
    ]


def copies(pairs, sems):
    moves = [pltpu.make_async_copy(a, b, sems.at[i]) for i, (a, b) in enumerate(pairs)]
    for move in moves:
        move.start()
    return moves


def place():
    tile, tiles = lax.axis_index("tile"), lax.axis_size("tile")
    return tile % 2 == 1, jnp.logical_or(tile == 0, tile == tiles - 1)


def across_lanes(a, b):
    return lax.dot_general(a, b, (((1,), (1,)), ((), ())), preferred_element_type=jnp.float32)


def half_spectrum(window, rows, side):
    high, low = halves(window[:, pl.ds(pl.multiple_of(side * MARGIN, MARGIN), MARGIN)])
    both = dot(rows[:WIDE], jnp.concatenate([high, low], 1))
    z = both[:, :MARGIN] + both[:, MARGIN:] + dot(rows[WIDE:], high)
    columns = rows[:, pl.ds(pl.multiple_of(side * MARGIN, MARGIN), MARGIN)]
    both = across_lanes(
        jnp.concatenate(halves(z), 1), jnp.concatenate([columns, columns], 1)
    )
    w = both[:, :WIDE] + both[:, WIDE:]
    return (w[:BAND] + turn(w[BAND:])) * signs((BAND, WIDE))


def analyze_kernel(
    mask_hbm, rows_hbm, target_hbm, odd_out, mask, rows, target, sems
):
    odd, _ = place()
    moves = copies(
        [
            (mask_hbm, mask),
            (rows_hbm, rows),
            (target_hbm, target),
        ],
        sems,
    )
    for move in moves[:2]:
        move.wait()
    odd_out[...] = half_spectrum(mask, rows, jnp.where(odd, 1, 0))
    for move in moves[2:]:
        move.wait()


def own_kernel(mask, odd_out, rows, even_out, own):
    odd, _ = place()
    even = half_spectrum(mask, rows, jnp.where(odd, 0, 1))
    even_out[...] = even
    own[...] = (even + odd_out[...]) * signs((BAND, WIDE))


def prepare_kernel(
    after, target, table_hbm, index_hbm, weight_hbm, dose_hbm, mixed, goal, table, index, weight, dose, sems
):
    moves = copies(
        strips(table_hbm, table, TABLE // 2) + [(index_hbm, index), (weight_hbm, weight), (dose_hbm, dose)],
        sems,
    )
    goal[...] = 1.0 - 2.0 * target[...]
    for move in moves:
        move.wait()
    for condition in range(CONDS):
        entry = index[condition]
        for k in range(KERN):
            scale = jnp.sqrt(
                jnp.full((1, WIDE), 0.5 * steepness * dose[entry] * weight[k, entry])
            ) * (1.0 / (NPAD * NPAD))
            for part in range(2):
                kernel = table[entry, k, part]
                doubled = jnp.concatenate([kernel, kernel], 1)
                mixed[condition * KERN + k, part] = doubled * scale


def join_kernel(own, odd_in, joined):
    _, alone = place()
    joined[...] = own[...] + jnp.where(alone, 0.0, odd_in[...])


def window_kernel(joined, even_in, goal, mixed, rows, tables, resist, grad, odd_out):
    points, points_t, turned_high, turned_low, finer, finer_t, back_both = table_parts(tables)
    spec = joined[...] + even_in[...]
    turned = turn(spec)
    out_high = jnp.concatenate([rows[:WIDE], turned_high[...]], 1)
    out_low = jnp.concatenate([rows[WIDE:], turned_low[...]], 1)
    out_twice = jnp.concatenate([out_high, out_high], 0)
    conditions = range(CONDS)

    def coarse_rows(condition):
        group = range(condition * KERN, (condition + 1) * KERN)
        top = jnp.concatenate([mixed[i, 0] * spec + mixed[i, 1] * turned for i in group], 1)
        bottom = jnp.concatenate([mixed[i, 1] * spec - mixed[i, 0] * turned for i in group], 1)
        high, low = halves(jnp.concatenate([top, bottom], 0))
        return dot(points_t[...], jnp.concatenate([high, high], 0)) + dot(points_t[:, :WIDE], low)

    def coarse_field(y):
        y = jnp.concatenate([y[:, k * WIDE : (k + 1) * WIDE] for k in range(KERN)], 0)
        high, low = halves(y)
        return dot(jnp.concatenate([high, low], 1), out_twice) + dot(high, out_low)

    def finer_rows(f):
        squares = f * f
        power = sum(
            squares[k * COARSE : (k + 1) * COARSE, c]
            for k in range(KERN)
            for c in (slice(0, CORE), slice(CORE, 2 * CORE))
        )
        high, low = halves(power - 0.5 * steepness * threshold)
        both = jnp.concatenate([high, low], 1)
        both = dot(finer[...], jnp.concatenate([both, both], 0))
        return both[:, :CORE] + both[:, CORE:]

    def print_and_drive(condition, power):
        t = jnp.tanh(power)
        resist[condition] = 0.5 + 0.5 * t
        return (t + goal[...]) * (1.0 - t * t)

    def coarser_rows(drive):
        high, low = halves(drive)
        both = dot(finer_t[:COARSE], jnp.concatenate([high, low], 1))
        return both[:, :CORE] + both[:, CORE:] + dot(finer_t[COARSE:], high)

    def back_columns(drive, f):
        drive = jnp.concatenate([drive, drive], 1)
        high, low = halves(jnp.concatenate([drive] * KERN, 0) * f)
        both = dot(high, back_both[...])
        q = both[:, :WIDE] + both[:, WIDE:] + dot(low, back_both[:, :WIDE])
        return jnp.concatenate([q[k * COARSE : (k + 1) * COARSE] for k in range(KERN)], 1)

    def back_rows(q):
        high, low = halves(q)
        return dot(points[...], jnp.concatenate([high, high], 0)) + dot(points[:, :COARSE], low)

    y = [coarse_rows(c) for c in conditions]
    fields = [coarse_field(x) for x in y]
    power = [finer_rows(f) for f in fields]
    drive = [print_and_drive(c, power[c]) for c in conditions]
    drive = [coarser_rows(x) for x in drive]
    q = [back_columns(drive[c], fields[c]) for c in conditions]
    u = [back_rows(x) for x in q]
    straight = jnp.zeros((BAND, WIDE), jnp.float32)
    crossed = jnp.zeros((BAND, WIDE), jnp.float32)
    for i in range(PAIRS):
        c = slice(i % KERN * WIDE, (i % KERN + 1) * WIDE)
        top, bottom = u[i // KERN][:BAND, c], u[i // KERN][BAND:, c]
        straight = straight + (mixed[i, 0] * top + mixed[i, 1] * bottom)
        crossed = crossed + (mixed[i, 0] * bottom - mixed[i, 1] * top)
    total = 2.0 * (straight + turn(crossed))
    grad[...] = total
    odd_out[:BAND] = total
    odd_out[BAND:] = total[: odd_out.shape[0] - BAND]


def synthesize(spec, rows, rows_t, side, out):
    both = jnp.concatenate(halves(stacked(spec)), 1)
    y = dot(rows_t[...], jnp.concatenate([both, both], 0))
    y = jnp.concatenate(halves(y[:, :WIDE] + y[:, WIDE:]), 1)
    c = pl.ds(pl.multiple_of(side * MARGIN, MARGIN), MARGIN)
    columns = jnp.concatenate([rows[:WIDE, c], rows[WIDE:, c]], 1)
    both = dot(y, jnp.concatenate([columns, columns], 0))
    out[...] = both[:, :MARGIN] + both[:, MARGIN:]


def store_kernel(resist, resist_hbm, sems):
    for move in copies([(resist, resist_hbm)], sems):
        move.wait()


def beside_kernel(own, even_in, rows, tables, half):
    odd, _ = place()
    spec = own[...] + even_in[...] * signs((BAND, WIDE))
    synthesize(spec, rows, table_parts(tables)[-1].at[:CORE], jnp.where(odd, 0, 1), half)


def across_kernel(own, odd_in, rows, tables, half, gradient_hbm, out, sems):
    odd, alone = place()
    side = jnp.where(odd, 1, 0)

    def columns(side):
        return gradient_hbm.at[:, pl.ds(pl.multiple_of(side * MARGIN, MARGIN), MARGIN)]

    moves = copies([(half, columns(1 - side))], sems)
    extra = jnp.where(alone, 0.0, odd_in[:BAND] * signs((BAND, WIDE)))
    synthesize(own[...] + extra, rows, table_parts(tables)[-1].at[:CORE], side, out)
    moves += copies([(out, columns(side))], sems.at[1:])
    for move in moves:
        move.wait()


def pinned(*arrays):
    return [pltpu.with_memory_space_constraint(jnp.asarray(a), pltpu.HBM) for a in arrays]


SPACES = {"v": pltpu.VMEM, "h": pltpu.HBM, "s": pltpu.SMEM}


def call(kernel, ins, outs, scratch=(), aliases=None, flops=10**6):
    shapes = [jax.ShapeDtypeStruct(shape, dtype) for _, shape, dtype in outs]
    specs = [pl.BlockSpec(memory_space=SPACES[o[0]]) for o in outs]
    return pl.pallas_call(
        kernel,
        out_shape=shapes if len(shapes) > 1 else shapes[0],
        in_specs=[pl.BlockSpec(memory_space=SPACES[i]) for i in ins],
        out_specs=specs if len(specs) > 1 else specs[0],
        scratch_shapes=list(scratch),
        input_output_aliases=aliases or {},
        compiler_params=pltpu.CompilerParams(vmem_limit_bytes=16 << 20),
        cost_estimate=pl.CostEstimate(flops=flops, bytes_accessed=1 << 16, transcendentals=0),
    )


def partners(windows, tiles):
    even = [(w * tiles + i, w * tiles + (i ^ 1)) for w in range(windows) for i in range(tiles)]
    odd = []
    for w in range(windows):
        base = w * tiles
        for i in range(1, tiles - 1, 2):
            odd += [(base + i, base + i + 1), (base + i + 1, base + i)]
        other = w ^ 1 if (w ^ 1) < windows else w
        for i in (0, tiles - 1):
            odd.append((base + i, other * tiles + i))
    return even, odd


def local(mask, target, kernel_table, kernel_weight, dose_table, condition_index):
    rows_table = np.concatenate(parts(waves(np.arange(MARGIN, MARGIN + CORE))), 0)
    tables = later_tables(rows_table)
    even, odd = partners(lax.axis_size("win"), lax.axis_size("tile"))
    over = ("win", "tile")
    f32, bf16 = jnp.float32, jnp.bfloat16
    small = ("v", (BAND, WIDE), f32)
    square = (CORE, CORE)
    dma, smem = pltpu.SemaphoreType.DMA, pltpu.SMEM
    half = ("v", (CORE, MARGIN), f32)
    to_odd, window, rows, goal = call(
        analyze_kernel,
        "hhh",
        [small, ("v", square, f32), ("v", square, bf16)] + [("v", x.shape, f32) for x in (target,)],
        [dma((3,))],
    )(*pinned(mask, rows_table, target))
    from_odd = lax.ppermute(to_odd, over, odd)
    to_even, own = call(own_kernel, "vvv", [small, small])(window, to_odd, rows)
    from_even = lax.ppermute(to_even, over, even)
    mixed, goal = call(
        prepare_kernel,
        "vvhhhh",
        [("v", (PAIRS, 2, BAND, WIDE), f32), ("v", square, f32)],
        [
            pltpu.VMEM((TABLE, KERN, 2, BAND, BAND), f32),
            smem((CONDS,), jnp.int32),
            smem((KERN, TABLE), f32),
            smem((TABLE,), f32),
            dma((5,)),
        ],
    )(own, goal, *pinned(kernel_table, condition_index, kernel_weight.T, dose_table))
    joined = call(join_kernel, "vv", [small])(own, from_odd)
    resist, grad, to_odd = call(
        window_kernel,
        "v" * 6,
        [("v", (CONDS, CORE, CORE), f32), small, ("v", (BAND + 8, WIDE), f32)],
    )(joined, from_even, goal, mixed, rows, tables)
    from_odd = lax.ppermute(to_odd, over, odd)
    from_even = lax.ppermute(grad, over, even)
    resist = call(store_kernel, "v", [("h", (CONDS, CORE, CORE), f32)], [dma((1,))])(resist)
    made = call(beside_kernel, "vvvv", [half])(grad, from_even, rows, tables)
    gradient = call(
        across_kernel,
        "vvvvv",
        [("h", square, f32)],
        [pltpu.VMEM((CORE, MARGIN), f32), dma((2,))],
    )(grad, from_odd, rows, tables, made)
    return (resist, gradient)


def solution(mesh):
    return jax.shard_map(
        local,
        mesh=mesh,
        in_specs=(P("win", "tile"), P("win", "tile"), P(), P(), P(), P()),
        out_specs=(P(None, "win", "tile"), P("win", "tile")),
        check_vma=False,
    )
```
